32 devices in a mesh: groups: 2 (over x), mesh: 16 (over z, y, core).
Axes of the slice: x: 2, y: 2, z: 4, core: 2. Of those that a mesh axis runs over, the one named last changes fastest.
Arguments:
- state: float32 [3, 64, 32768], P(None, None, ('groups', 'mesh')), parts along dimension 2, may hold values from -6 to 6
- depth: float32 [32768], P(('groups', 'mesh')), parts along dimension 0, may hold values from 0.5 to 4
- coef: float32 [2, 6, 32768], P(None, None, ('groups', 'mesh')), parts along dimension 2, may hold values from -2 to 2
- wet_faces: int32 [6, 32768], P(None, ('groups', 'mesh')), parts along dimension 1, may hold values 0 or 1
- conn: int32 [6, 32768], P(None, ('groups', 'mesh')), parts along dimension 1, may hold values from 0 to 1535, as said below
- send_list: int32 [2, 8192], P(None, ('groups', 'mesh')), parts along dimension 1, may hold values from 0 to 1023, as said below
- obs_nodes: int32 [3, 32768], P(None, ('groups', 'mesh')), parts along dimension 1, may hold values from 0 to 1023
- obs_weight: float32 [3, 32768], P(None, ('groups', 'mesh')), parts along dimension 1, may hold values from 0 to 1, as said below
- obs_value: float32 [32768], P(('groups', 'mesh')), parts along dimension 0, may hold values from -9 to 9
- obs_error: float32 [32768], P(('groups', 'mesh')), parts along dimension 0, may hold values from 0.5 to 2
- loc_ids: int32 [32, 512], P(('groups', 'mesh')), parts along dimension 0, may hold values from 0 to 16383, as said below
- loc_len: int32 [32], P(('groups', 'mesh')), parts along dimension 0, may hold values from 64 to 512, as said below
- loc_weight: float32 [32, 512], P(('groups', 'mesh')), parts along dimension 0, may hold values from 0.05 to 1
Outputs:
- analysis: float32 [3, 64, 32768], P(None, None, ('groups', 'mesh')), parts along dimension 2
The draws below stay inside these ranges and needn't reach their ends.
There are 2 independent parts, one for each index of `groups`. The reference program is written for one: setup_inputs(seed, part) draws one part's arguments, and reference() takes and returns one part's arrays. A program takes and returns all parts, laid end to end along the dimension named above; each array names one. Nothing has to cross between parts.
Inputs may be any that keep to these rules, and one draw needn't show every extreme that they name: `conn`: for each partition: below 1024 a local node; 1024 + p is slot p of the lower partition's list toward it, 1280 + p slot p of the higher partition's list toward it; the first partition names no lower slot and the last no higher one. `send_list`: each partition's two lists hold 256 distinct local node numbers each. `obs_weight`: the three weights of an observation are positive and sum to one. `loc_ids`: the entries of a patch's list are distinct and name observations held by the patch's partition or the two beside it. `loc_len`: patch 0 has a list of length 512.
All inputs are finite; a program needn't handle non-finite values. No bound on the sum of `wet_faces` on one device may be relied on, other than what follows from the above.
Results may differ from the reference program's by a relative error of at most 0.0003.
Values sent between devices are 32-bit elements; how exact they have to be, the bound alone decides.
No kernel may reach another device: no remote copies, remote signals or barrier semaphores. Data moves between devices by JAX's collectives and lax.ppermute only.
A program may use at most 64 MiB of HBM per device.

```python
import math
import jax
import jax.numpy as jnp
from jax import lax

MEM = 64
NB = 6
VERTICES_PER_AREA = 1024
PATCH_DEV = 1
HALO = 256
OBS_DEV = 1024
LOC = 512
STEPS = 2
NODE_DEV = 1024
NODES = 16384
ASSIMILATE_AREAS = 16
OBS = 16384
N_MESH = 16


def draw_conn(key, part):
    column = jnp.arange(NODES, dtype=jnp.int32)
    device = column // NODE_DEV
    local = column % NODE_DEV
    keys = jax.random.split(jax.random.fold_in(key, 11), 3)
    kind = jax.random.randint(keys[0], (NB, NODES), 0, 8)
    offset = jax.random.randint(keys[1], (NB, NODES), -16, 17)
    place = jax.random.randint(keys[2], (NB, NODES), 0, HALO)
    nearby = jnp.clip(local[None, :] + offset, 0, NODE_DEV - 1)
    lower_ok = (kind == 0) & (device[None, :] > 0)
    upper_ok = (kind == 1) & (device[None, :] < N_MESH - 1)
    assimilated_output = jnp.where(lower_ok, NODE_DEV + place, jnp.where(upper_ok, NODE_DEV + HALO + place, nearby))
    return assimilated_output.astype(jnp.int32)


def draw_send_list(key, part):
    keys = jax.random.split(jax.random.fold_in(key, 23), 2 * N_MESH)
    lists = jax.vmap(lambda single: jax.random.permutation(single, NODE_DEV)[:HALO])(keys)
    return lists.reshape(2, N_MESH * HALO).astype(jnp.int32)


def draw_obs_weight(key, part):
    inner = jax.random.fold_in(key, 53)
    raw = jax.random.uniform(inner, (3, OBS), jnp.float32, 0.2, 1.0)
    return raw / jnp.sum(raw, axis=0, keepdims=True)


def draw_loc_ids(key, part):
    width = 3 * OBS_DEV
    keys = jax.random.split(jax.random.fold_in(key, 37), ASSIMILATE_AREAS)
    device = jnp.arange(ASSIMILATE_AREAS, dtype=jnp.int32) // PATCH_DEV

    def single(subkey, owner):
        ranks = jax.random.permutation(subkey, width).astype(jnp.int32)
        candidate = jnp.arange(width, dtype=jnp.int32)
        target = owner + candidate // OBS_DEV - 1
        outside = ((target < 0) | (target >= N_MESH)).astype(jnp.int32)
        order = jnp.argsort(ranks + outside * width).astype(jnp.int32)
        return (owner - 1) * OBS_DEV + order[:LOC]
    return jax.vmap(single)(keys, device).astype(jnp.int32)


def draw_loc_len(key, part):
    lengths = jax.random.randint(jax.random.fold_in(key, 41), (ASSIMILATE_AREAS,), LOC // 8, LOC + 1)
    first = jnp.arange(ASSIMILATE_AREAS, dtype=jnp.int32) == 0
    return jnp.where(first, LOC, lengths).astype(jnp.int32)


def place_ends(drawn, key, least, largest):
    shape = drawn.shape
    spot = [jax.random.randint(jax.random.fold_in(key, axis), (), 0, shape[axis]) for axis in range(len(shape))]
    drawn = drawn.at[tuple(spot)].set(least)
    longest = shape.index(max(shape))
    spot[longest] = (spot[longest] + 1) % shape[longest]
    return drawn.at[tuple(spot)].set(largest)


def block_levels(own_key, extent, cuts, least, top_value):
    def one(position, blocks):
        steps = jax.random.uniform(jax.random.fold_in(jax.random.fold_in(own_key, 6), position), (blocks,), jnp.float32, least / len(cuts), top_value / len(cuts))
        return jnp.repeat(jnp.exp(steps), extent[position] // blocks).reshape((-1,) + (1,) * (len(extent) - position - 1))

    factor_of = one(*cuts[0])
    for cut in cuts[1:]:
        factor_of = factor_of * one(*cut)
    return factor_of


def scatter_about(own_key, extent, scale, reach, cuts=(), held_as=jnp.bfloat16):
    values = jax.random.normal(own_key, extent, jnp.float32) * scale
    if len(cuts) > 0:
        values = block_levels(own_key, extent, cuts, -0.22, 0.18) * values
    return jnp.clip(values, min=-reach, max=reach).astype(held_as)


def setup_inputs(seed: int = 0, part: int = 0) -> dict:
    seeds = jax.random.split(jax.random.key(seed), 14)
    own_keys = jax.random.split(jax.random.fold_in(seeds[13], part), 14)
    return {
        "state": scatter_about(own_keys[0], (3, MEM, NODES), 1.0, 6.0, ((2, 16),), jnp.float32),
        "depth": jnp.clip(jnp.exp(math.log(4.0) - 2.0794415 * jax.random.uniform(own_keys[1], (NODES,), jnp.float32) ** block_levels(own_keys[1], (NODES,), ((0, 16),), -0.2, 0.2)), 0.5, 4.0),
        "coef": scatter_about(own_keys[2], (2, NB, NODES), 0.4, 2.0, ((2, 16),), jnp.float32),
        "wet_faces": place_ends((jax.random.randint(own_keys[3], (NB, NODES), 0, 8) < 7).astype(jnp.int32), jax.random.fold_in(own_keys[3], 1), 0, 1),
        "conn": draw_conn(jax.random.fold_in(jax.random.fold_in(seeds[13], part), 71), part),
        "send_list": draw_send_list(jax.random.fold_in(jax.random.fold_in(seeds[13], part), 71), part),
        "obs_nodes": place_ends(jax.random.randint(own_keys[6], (3, OBS), 0, NODE_DEV), jax.random.fold_in(own_keys[6], 1), 0, NODE_DEV - 1).astype(jnp.int32),
        "obs_weight": draw_obs_weight(jax.random.fold_in(jax.random.fold_in(seeds[13], part), 71), part),
        "obs_value": scatter_about(own_keys[8], (OBS,), 1.5, 9.0, ((0, 16),), jnp.float32),
        "obs_error": jnp.clip(jnp.exp(math.log(2.0) - 1.3862944 * jax.random.uniform(own_keys[9], (OBS,), jnp.float32) ** block_levels(own_keys[9], (OBS,), ((0, 16),), -0.2, 0.2)), 0.5, 2.0),
        "loc_ids": draw_loc_ids(jax.random.fold_in(jax.random.fold_in(seeds[13], part), 71), part),
        "loc_len": draw_loc_len(jax.random.fold_in(jax.random.fold_in(seeds[13], part), 71), part),
        "loc_weight": jnp.clip(0.05 + 0.95 * jax.random.uniform(own_keys[12], (ASSIMILATE_AREAS, LOC), jnp.float32) ** block_levels(own_keys[12], (ASSIMILATE_AREAS, LOC), ((0, 16),), -0.2, 0.2), 0.05, 1.0),
    }


DT = 0.1
TOPMOST = lax.Precision.HIGHEST

def spread(field, lists):
    lead = field.shape[:-2]

    def pick(chosen):
        return jnp.take_along_axis(field, jnp.broadcast_to(chosen, lead + chosen.shape), axis=-1)
    to_lower = pick(lists[0])
    to_upper = pick(lists[1])
    blank = jnp.zeros_like(to_lower[..., :1, :])
    from_lower = jnp.concatenate([blank, to_upper[..., :-1, :]], axis=-2)
    from_upper = jnp.concatenate([to_lower[..., 1:, :], blank], axis=-2)
    return jnp.concatenate([field, from_lower, from_upper], axis=-1)

def fetch(extended, chosen):
    lead = extended.shape[:-2]
    return jnp.take_along_axis(extended, jnp.broadcast_to(chosen, lead + chosen.shape), axis=-1)

def mapping_operator(advance_prior_model, collected_lines, departure_lines, coefficient_lines):
    ensemble_fields = collected_lines.shape[0]
    prior_average = lax.optimization_barrier(jnp.mean(advance_prior_model, axis=1, keepdims=True))
    dispersion_piece = advance_prior_model - prior_average
    weighted = collected_lines * coefficient_lines[None]
    inner_product_table = jnp.einsum('mpl,npl->pmn', weighted, collected_lines, precision=TOPMOST)
    unit = jnp.eye(ensemble_fields, dtype=jnp.float32)
    inner_product_table = inner_product_table + (ensemble_fields - 1.0) * unit
    linear_system_source = jnp.einsum('mpl,pl->pm', collected_lines, coefficient_lines * departure_lines, precision=TOPMOST)
    lower = jnp.linalg.cholesky(inner_product_table)
    inv_lower = lax.linalg.triangular_solve(lower, jnp.broadcast_to(unit, inner_product_table.shape), left_side=True, lower=True)
    halfway = lax.linalg.triangular_solve(lower, linear_system_source[..., None], left_side=True, lower=True)
    mean_w = lax.linalg.triangular_solve(lower, halfway, left_side=True, lower=True, transpose_a=True)[..., 0]
    blending_coefficients = mean_w[:, :, None] + math.sqrt(ensemble_fields - 1.0) * jnp.swapaxes(inv_lower, 1, 2)
    return prior_average + jnp.einsum('hwz,vwhx->vzhx', blending_coefficients, dispersion_piece, precision=TOPMOST)

def reference(state, depth, coef, wet_faces, conn, send_list, obs_nodes, obs_weight, obs_value, obs_error, loc_ids, loc_len, loc_weight):
    ensemble_fields = state.shape[1]
    parts = N_MESH
    shaped = state.reshape(3, ensemble_fields, parts, NODE_DEV)
    free_elevation = shaped[0]
    discharge_rate = shaped[1:]
    lists = send_list.reshape(2, parts, HALO)
    links = conn.reshape(NB, parts, NODE_DEV)
    faces = wet_faces.astype(jnp.float32).reshape(NB, parts, NODE_DEV)
    slopes = coef.reshape(2, NB, parts, NODE_DEV)
    height = depth.reshape(parts, NODE_DEV)
    for section in range(STEPS):
        extended = spread(discharge_rate, lists)
        divergence = jnp.zeros_like(free_elevation)
        for slot in range(NB):
            nearby = fetch(extended, links[slot])
            divergence = divergence + faces[slot] * (slopes[0, slot] * (nearby[0] - discharge_rate[0]) + slopes[1, slot] * (nearby[1] - discharge_rate[1]))
        free_elevation = free_elevation - DT * height * divergence
        ext_level = spread(free_elevation, lists)
        slope_east = jnp.zeros_like(free_elevation)
        slope_north = jnp.zeros_like(free_elevation)
        for slot in range(NB):
            change = fetch(ext_level, links[slot]) - free_elevation
            slope_east = slope_east + faces[slot] * slopes[0, slot] * change
            slope_north = slope_north + faces[slot] * slopes[1, slot] * change
        discharge_rate = jnp.stack([discharge_rate[0] - DT * slope_east, discharge_rate[1] - DT * slope_north])
    flat_level = free_elevation.reshape(ensemble_fields, NODES)
    owners = jnp.arange(OBS, dtype=jnp.int32) // OBS_DEV * NODE_DEV
    observed = jnp.zeros((ensemble_fields, OBS), jnp.float32)
    for corner in range(3):
        observed = observed + obs_weight[corner] * jnp.take(flat_level, obs_nodes[corner] + owners, axis=1)
    obs_mean = lax.optimization_barrier(jnp.mean(observed, axis=0))
    anomalies = observed - obs_mean
    innovation = obs_value - obs_mean
    numeric_accuracy = 1.0 / (obs_error * obs_error)
    collected_lines = jnp.take(anomalies, loc_ids, axis=1)
    departure_lines = jnp.take(innovation, loc_ids, axis=0)
    prec_list = jnp.take(numeric_accuracy, loc_ids, axis=0)
    live = (jnp.arange(LOC, dtype=jnp.int32)[None, :] < loc_len[:, None]).astype(jnp.float32)
    coefficient_lines = prec_list * loc_weight * live
    advance_prior_model = jnp.stack([free_elevation, discharge_rate[0], discharge_rate[1]]).reshape(3, ensemble_fields, ASSIMILATE_AREAS, VERTICES_PER_AREA)
    assimilated_output = mapping_operator(advance_prior_model, collected_lines, departure_lines, coefficient_lines)
    return assimilated_output.reshape(3, ensemble_fields, NODES)
```

```python
import functools
import math

import jax
import jax.numpy as jnp
from jax import lax
from jax.experimental import pallas as pl
from jax.experimental.pallas import tpu as pltpu
from jax.sharding import PartitionSpec as P

STEPS = 2
DT = 0.1
LANES = 128
ROWS = 8
F32 = jnp.float32
BF16 = jnp.bfloat16
TOPMOST = lax.Precision.HIGHEST


def halves(value):
    high = value.astype(BF16)
    return high, (value - high.astype(F32)).astype(BF16)


def stacked(value):
    high, low = halves(value)
    return jnp.concatenate([high, low], axis=0)


def product(stack, high, low):
    rows = stack.shape[0] // 2
    total = jnp.dot(stack, high, preferred_element_type=F32) + jnp.dot(stack, low, preferred_element_type=F32)
    return total[:rows] + total[rows:]


def pick_lanes(sources, indices, targets):
    rows, extent = sources.shape
    plans = []
    for index, target in zip(indices, targets):
        for start in range(0, index.shape[1], LANES):
            wide = jnp.broadcast_to(index[:, start : start + LANES], (ROWS, LANES))
            plans.append((wide & (LANES - 1), wide >> 7, target, start))

    def group(step, carry):
        first = pl.multiple_of(step * ROWS, ROWS)
        for lane, tile, (ref, row0, col0), start in plans:
            total = jnp.zeros((ROWS, LANES), F32)
            for place in range(extent // LANES):
                block = sources[pl.ds(first, ROWS), place * LANES : (place + 1) * LANES]
                found = jnp.take_along_axis(block, lane, axis=1, mode="promise_in_bounds")
                total = jnp.where(tile == place, found, total)
            ref[pl.ds(row0 + first, ROWS), col0 + start : col0 + start + LANES] = total
        return carry

    lax.fori_loop(0, rows // ROWS, group, 0, unroll=2)


def merged(targets, weights):
    targets = list(targets)
    weights = [list(group) for group in weights]
    count = len(targets)
    for first in range(count):
        for second in range(first + 1, count):
            same = targets[first] == targets[second]
            for group in weights:
                group[first] = group[first] + jnp.where(same, group[second], 0.0)
                group[second] = jnp.where(same, 0.0, group[second])
    return weights


def build_operator(targets, weights, outputs, begin, extent, column):
    count = len(targets)
    tall = 2 * ROWS
    wanted = [jnp.broadcast_to(t - begin, (tall, LANES)).astype(jnp.int16) for t in targets]
    parts = []
    for group in weights:
        for w in group:
            high = w.astype(BF16).astype(F32)
            parts.append(
                (
                    jnp.broadcast_to(high, (tall, LANES)).astype(BF16),
                    jnp.broadcast_to(w - high, (tall, LANES)).astype(BF16),
                )
            )

    def block(step, rows):
        first = pl.multiple_of(step * tall, tall)
        values = [jnp.zeros((tall, LANES), BF16) for _ in range(2 * len(weights))]
        for slot in range(count - 1, -1, -1):
            hit = wanted[slot] == rows
            for g in range(len(weights)):
                high, low = parts[g * count + slot]
                values[2 * g] = jnp.where(hit, high, values[2 * g])
                values[2 * g + 1] = jnp.where(hit, low, values[2 * g + 1])
        for value, ref in zip(values, outputs):
            ref[pl.ds(first, tall), column : column + LANES] = value
        return rows + jnp.int16(tall)

    start = lax.broadcasted_iota(jnp.int32, (tall, LANES), 0).astype(jnp.int16)
    lax.fori_loop(0, extent // tall, block, start, unroll=4)


def send_flow_kernel(state, lists, ids, lower, upper):
    members, width = state.shape[1], lists.shape[1]
    for which, ref in enumerate((lower, upper)):
        for part in range(2):
            pick_lanes(state.at[1 + part], [lists[which : which + 1, :]], [(ref, part * members, 0)])
        block = jnp.zeros((ref.shape[0] - 2 * members, width), F32)
        row = lax.broadcasted_iota(jnp.int32, block.shape, 0)
        for piece in range(ids.shape[1] // width):
            numbers = ids[:, piece * width : (piece + 1) * width].astype(F32)
            block = jnp.where(row == piece, jnp.broadcast_to(numbers, block.shape), block)
        ref[2 * members :, :] = block


def prepare_kernel(state, coef, wet, conn, eh, el, nh, nl, geh, gel, gnh, gnl, totals, partial):
    slots, nodes = conn.shape
    ghosts = geh.shape[0]
    for column in range(0, nodes, LANES):
        cut = slice(column, column + LANES)
        targets = [conn[s : s + 1, cut] for s in range(slots)]
        faces = [wet[s : s + 1, cut].astype(F32) for s in range(slots)]
        weights = [[faces[s] * coef[d, s : s + 1, cut] for s in range(slots)] for d in range(2)]
        for d in range(2):
            totals[d : d + 1, cut] = sum(weights[d][1:], weights[d][0])
        weights = merged(targets, weights)
        build_operator(targets, weights, (eh, el, nh, nl), 0, nodes, column)
        build_operator(targets, weights, (geh, gel, gnh, gnl), nodes, ghosts, column)
    partial[...] = (
        product(stacked(state[1]), eh[...], el[...])
        + product(stacked(state[2]), nh[...], nl[...])
        - state[1] * totals[0:1, :]
        - state[2] * totals[1:2, :]
    )


def ghost_flow(lower, upper, part, members):
    rows = slice(part * members, (part + 1) * members)
    return jnp.concatenate([lower[rows, :], upper[rows, :]], axis=1)


def level_kernel(level, partial, depth, lower, upper, geh, gel, gnh, gnl, lists, new_level, to_lower, to_upper):
    members = level.shape[0]
    divergence = (
        partial[...]
        + product(stacked(ghost_flow(lower, upper, 0, members)), geh[...], gel[...])
        + product(stacked(ghost_flow(lower, upper, 1, members)), gnh[...], gnl[...])
    )
    new_level[...] = level[...] - DT * depth[...] * divergence
    pick_lanes(new_level, [lists[0:1, :], lists[1:2, :]], [(to_lower, 0, 0), (to_upper, 0, 0)])


def last_level_kernel(
    level, partial, depth, lower, upper, geh, gel, gnh, gnl, lists, sampling_high, sampling_low, new_level, to_lower, to_upper
):
    members, width = level.shape[0], lists.shape[1]
    entries = to_lower.shape[1] - width
    level_kernel(level, partial, depth, lower, upper, geh, gel, gnh, gnl, lists, new_level, to_lower, to_upper)
    seen = product(
        stacked(new_level[...]), sampling_high[:, : 2 * entries], sampling_low[:, : 2 * entries]
    )
    to_lower[:, width:] = seen[:, :entries]
    to_upper[:, width:] = seen[:, entries:]


def slope_kernel(level, eh, el, nh, nl, totals, east, north):
    stack = stacked(level[...])
    east[...] = product(stack, eh[...], el[...]) - level[...] * totals[0:1, :]
    north[...] = product(stack, nh[...], nl[...]) - level[...] * totals[1:2, :]


def sampling_kernel(
    place, lower, upper, ids, obs_nodes, obs_weight, obs_value, obs_error, high, low, tables, numbers, scratch, found
):
    members_rows = lower.shape[0]
    entries = ids.shape[1]
    width = lower.shape[1]
    obs_count = obs_nodes.shape[1]
    base = place[0] * obs_count
    corners = obs_nodes.shape[0]
    precision = 1.0 / (obs_error[...] * obs_error[...])
    scratch[0:corners, :] = obs_nodes[...].astype(F32)
    scratch[corners : 2 * corners, :] = obs_weight[...]
    scratch[2 * corners : 2 * corners + 1, :] = obs_value[...]
    scratch[2 * corners + 1 : 2 * corners + 2, :] = precision
    first = members_rows - ROWS
    for piece in range(entries // width):
        cut = slice(piece * width, (piece + 1) * width)
        numbers[0:1, cut] = lower[first + piece : first + piece + 1, :].astype(jnp.int32)
        numbers[1:2, cut] = upper[first + piece : first + piece + 1, :].astype(jnp.int32)
    numbers[2:3, :] = ids[...]
    for owner in range(3):
        for start in range(0, entries, LANES):
            index = numbers[owner : owner + 1, start : start + LANES] - base
            own = (index >= 0) & (index < obs_count)
            index = jnp.where(own, index, 0)
            pick_lanes(scratch, [index], [(found, 0, 0)])
            targets = [found[c : c + 1, :].astype(jnp.int32) for c in range(corners)]
            weights = [jnp.where(own, found[corners + c : corners + c + 1, :], 0.0) for c in range(corners)]
            weights = merged(targets, [weights])
            build_operator(targets, weights, (high, low), 0, high.shape[0], owner * entries + start)
            for extra in range(2):
                row = 2 * corners + extra
                tables[2 * owner + extra : 2 * owner + extra + 1, start : start + LANES] = jnp.where(
                    own, found[row : row + 1, :], 0.0
                )


def flow_kernel(
    flow, east, north, lower, upper, geh, gel, gnh, gnl, lists, tables, new_flow, to_lower, to_upper
):
    members, width = east.shape[0], lists.shape[1]
    stack = stacked(jnp.concatenate([lower[...], upper[...]], axis=1))
    new_flow[0] = flow[0] - DT * (east[...] + product(stack, geh[...], gel[...]))
    new_flow[1] = flow[1] - DT * (north[...] + product(stack, gnh[...], gnl[...]))
    entries = tables.shape[1]
    for which, ref in enumerate((to_lower, to_upper)):
        for part in range(2):
            pick_lanes(new_flow.at[part], [lists[which : which + 1, :]], [(ref, part * members, 0)])
        block = jnp.zeros((ref.shape[0] - 2 * members, width), F32)
        row = lax.broadcasted_iota(jnp.int32, block.shape, 0)
        pieces = entries // width
        for extra in range(2):
            for piece in range(pieces):
                values = tables[2 * which + extra : 2 * which + extra + 1, piece * width : (piece + 1) * width]
                block = jnp.where(row == extra * pieces + piece, jnp.broadcast_to(values, block.shape), block)
        ref[2 * members :, :] = block


def divergence_kernel(flow, eh, el, nh, nl, totals, partial):
    partial[...] = (
        product(stacked(flow[0]), eh[...], el[...])
        + product(stacked(flow[1]), nh[...], nl[...])
        - flow[0] * totals[0:1, :]
        - flow[1] * totals[1:2, :]
    )


def last_slope_kernel(level, eh, el, nh, nl, totals, sampling_high, sampling_low, east, north, seen):
    slope_kernel(level, eh, el, nh, nl, totals, east, north)
    entries = seen.shape[1]
    seen[...] = product(
        stacked(level[...]), sampling_high[:, 2 * entries :], sampling_low[:, 2 * entries :]
    )


def inverse_factor(gram):
    size = gram.shape[0]
    row = lax.broadcasted_iota(jnp.int32, (size, size), 0)
    col = lax.broadcasted_iota(jnp.int32, (size, size), 1)
    unit = (row == col).astype(F32)
    table = jnp.concatenate([gram, unit], axis=1)
    blocks = [table[b : b + ROWS, :] for b in range(0, size, ROWS)]
    inner = lax.broadcasted_iota(jnp.int32, (ROWS, 2 * size), 0)
    for pivot in range(size):
        home, spot = divmod(pivot, ROWS)
        line = blocks[home][spot : spot + 1, :]
        scaled = line / line[:, pivot : pivot + 1]
        for b in range(home, len(blocks)):
            factor = blocks[b][:, pivot : pivot + 1]
            change = factor * scaled
            if b == home:
                change = jnp.where(inner > spot, change, 0.0)
            blocks[b] = blocks[b] - change
    table = jnp.concatenate(blocks, axis=0)
    diagonal = jnp.sum(jnp.where(row == col, table[:, :size], 0.0), axis=1, keepdims=True)
    return table[:, size:] * lax.rsqrt(diagonal)


def analysis_kernel(
    length, flow, level, east, north, seen, lower, upper, tables, early_lower, early_upper, loc_weight,
    geh, gel, gnh, gnl, out, fields,
):
    members, nodes = level.shape
    entries = seen.shape[1]
    width = lower.shape[1] - entries
    stack = stacked(jnp.concatenate([lower[:, :width], upper[:, :width]], axis=1))
    fields[0] = level[...]
    fields[1] = flow[0] - DT * (east[...] + product(stack, geh[...], gel[...]))
    fields[2] = flow[1] - DT * (north[...] + product(stack, gnh[...], gnl[...]))
    observed = seen[...] + lower[:, width:] + upper[:, width:]
    obs_mean = jnp.mean(observed, axis=0, keepdims=True)
    anomalies = observed - obs_mean
    pieces = entries // width
    first = early_lower.shape[0] - ROWS

    def received(extra):
        rows = [first + extra * pieces + piece for piece in range(pieces)]
        return jnp.concatenate([early_lower[r : r + 1, :] + early_upper[r : r + 1, :] for r in rows], axis=1)

    value = tables[4:5, :] + received(0)
    precision = tables[5:6, :] + received(1)
    live = lax.broadcasted_iota(jnp.int32, (1, entries), 1) < length[0]
    weight = jnp.where(live, precision * loc_weight[...], 0.0)
    pull = jnp.broadcast_to(weight * (value - obs_mean), (ROWS, entries))
    left = jnp.concatenate([anomalies * weight, pull], axis=0)
    sums = lax.dot_general(left, anomalies, (((1,), (1,)), ((), ())), precision=TOPMOST, preferred_element_type=F32)
    row = lax.broadcasted_iota(jnp.int32, (members, members), 0)
    col = lax.broadcasted_iota(jnp.int32, (members, members), 1)
    gram = sums[:members] + jnp.where(row == col, members - 1.0, 0.0)
    rhs = sums[members : members + 1]
    inverse = inverse_factor(gram)
    halfway = jnp.sum(inverse * rhs, axis=1, keepdims=True)
    mean_w = jnp.sum(inverse * halfway, axis=0, keepdims=True)
    blend = stacked(math.sqrt(members - 1.0) * inverse + mean_w)
    for part in range(3):
        field = fields[part]
        average = jnp.mean(field, axis=0, keepdims=True)
        high, low = halves(field - average)
        out[part] = average + product(blend, high, low)


def call(kernel, outs, args, name, scalars=0, scratch=(), flops=0):
    in_specs = [pl.BlockSpec(memory_space=pltpu.SMEM)] * scalars + [
        pl.BlockSpec(memory_space=pltpu.VMEM)
    ] * (len(args) - scalars)
    held = sum(math.prod(a.shape) * a.dtype.itemsize for a in list(args) + list(outs))
    return pl.pallas_call(
        kernel,
        out_shape=outs,
        in_specs=in_specs,
        out_specs=[pl.BlockSpec(memory_space=pltpu.VMEM)] * len(outs),
        scratch_shapes=scratch,
        name=name,
        cost_estimate=pl.CostEstimate(flops=flops, bytes_accessed=held, transcendentals=0),
    )(*args)


def shape(*dims, dtype=F32):
    return jax.ShapeDtypeStruct(dims, dtype)


def exchange(to_lower, to_upper):
    count = lax.axis_size("mesh")
    ahead = [(i, (i + 1) % count) for i in range(count)]
    back = [(target, source) for source, target in ahead]
    from_lower = lax.ppermute(to_upper, "mesh", ahead)
    from_upper = lax.ppermute(to_lower, "mesh", back)
    return from_lower, from_upper


def local(
    state,
    depth,
    coef,
    wet_faces,
    conn,
    send_list,
    obs_nodes,
    obs_weight,
    obs_value,
    obs_error,
    loc_ids,
    loc_len,
    loc_weight,
):
    members, nodes = state.shape[1:]
    width = send_list.shape[1]
    entries = loc_ids.shape[1]
    ghosts = 2 * width
    assert loc_ids.shape[0] == 1
    depth = depth[None]
    place = lax.axis_index("mesh").astype(jnp.int32)[None]
    work = 8 * members * nodes * nodes

    flow_rows = 2 * members + ROWS
    sent = call(
        send_flow_kernel, [shape(flow_rows, width)] * 2, [state, send_list, loc_ids], "send_flow"
    )
    from_lower, from_upper = exchange(*sent)
    big = [shape(nodes, nodes, dtype=BF16)] * 4
    small = [shape(ghosts, nodes, dtype=BF16)] * 4
    made = call(
        prepare_kernel,
        big + small + [shape(2, nodes), shape(members, nodes)],
        [state, coef, wet_faces, conn],
        "prepare",
        flops=4 * work,
    )
    operators, ghost_operators, totals, partial = made[:4], made[4:8], made[8], made[9]
    level, flow = state[0], state[1:]
    early = (from_lower, from_upper)
    for step in range(STEPS):
        last = step == STEPS - 1
        columns = width + (entries if last else 0)
        outs = [shape(members, nodes)] + [shape(members, columns)] * 2
        args = [level, partial, depth, from_lower, from_upper, *ghost_operators, send_list]
        if last:
            level, *sent = call(last_level_kernel, outs, args + [sampling_high, sampling_low], "last_level", flops=work)
        else:
            level, *sent = call(level_kernel, outs, args, "level", flops=work)
        from_lower, from_upper = exchange(*sent)
        slopes = [shape(members, nodes)] * 2
        args = [level, *operators, totals]
        if last:
            east, north, seen = call(
                last_slope_kernel,
                slopes + [shape(members, entries)],
                args + [sampling_high, sampling_low],
                "last_slope",
                flops=2 * work,
            )
            break
        east, north = call(slope_kernel, slopes, args, "slope", flops=2 * work)
        if step == 0:
            sampling_high, sampling_low, tables = call(
                sampling_kernel,
                [shape(nodes, 3 * entries, dtype=BF16)] * 2 + [shape(ROWS, entries)],
                [place, *early, loc_ids, obs_nodes, obs_weight, obs_value[None], obs_error[None]],
                "sampling",
                scalars=1,
                scratch=[
                    pltpu.VMEM((ROWS, entries), jnp.int32),
                    pltpu.VMEM((ROWS, obs_nodes.shape[1]), F32),
                    pltpu.VMEM((ROWS, LANES), F32),
                ],
                flops=work,
            )
        flow, *sent = call(
            flow_kernel,
            [shape(2, members, nodes)] + [shape(flow_rows, width)] * 2,
            [flow, east, north, from_lower, from_upper, *ghost_operators, send_list, tables],
            "flow",
            flops=work,
        )
        from_lower, from_upper = exchange(*sent)
        told = (from_lower, from_upper)
        (partial,) = call(
            divergence_kernel, [shape(members, nodes)], [flow, *operators, totals], "divergence", flops=2 * work
        )
    (out,) = call(
        analysis_kernel,
        [shape(3, members, nodes)],
        [
            loc_len,
            flow,
            level,
            east,
            north,
            seen,
            from_lower,
            from_upper,
            tables,
            *told,
            loc_weight,
            *ghost_operators,
        ],
        "analysis",
        scalars=1,
        scratch=[pltpu.VMEM((3, members, nodes), F32)],
        flops=work,
    )
    return out


def solution(mesh):
    spread = ("groups", "mesh")
    in_specs = (
        P(None, None, spread),
        P(spread),
        P(None, None, spread),
        P(None, spread),
        P(None, spread),
        P(None, spread),
        P(None, spread),
        P(None, spread),
        P(spread),
        P(spread),
        P(spread, None),
        P(spread),
        P(spread, None),
    )
    out_specs = P(None, None, spread)
    return jax.shard_map(local, mesh=mesh, in_specs=in_specs, out_specs=out_specs, check_vma=False)
```

```python
import functools
import math

import jax
import jax.numpy as jnp
from jax import lax
from jax.experimental import pallas as pl
from jax.experimental.pallas import tpu as pltpu
from jax.sharding import PartitionSpec as P

STEPS = 2
DT = 0.1
LANES = 128
ROWS = 8
F32 = jnp.float32
BF16 = jnp.bfloat16
TOPMOST = lax.Precision.HIGHEST


def halves(value):
    high = value.astype(BF16)
    return high, (value - high.astype(F32)).astype(BF16)


def stacked(value):
    high, low = halves(value)
    return jnp.concatenate([high, low], axis=0)


def product(stack, high, low):
    rows = stack.shape[0] // 2
    total = jnp.dot(stack, high, preferred_element_type=F32) + jnp.dot(stack, low, preferred_element_type=F32)
    return total[:rows] + total[rows:]


def pick_lanes(sources, indices, targets):
    rows, extent = sources.shape
    plans = []
    for index, target in zip(indices, targets):
        for start in range(0, index.shape[1], LANES):
            wide = jnp.broadcast_to(index[:, start : start + LANES], (ROWS, LANES))
            plans.append((wide & (LANES - 1), wide >> 7, target, start))

    def group(step, carry):
        first = pl.multiple_of(step * ROWS, ROWS)
        for lane, tile, (ref, row0, col0), start in plans:
            total = jnp.zeros((ROWS, LANES), F32)
            for place in range(extent // LANES):
                block = sources[pl.ds(first, ROWS), place * LANES : (place + 1) * LANES]
                found = jnp.take_along_axis(block, lane, axis=1, mode="promise_in_bounds")
                total = jnp.where(tile == place, found, total)
            ref[pl.ds(row0 + first, ROWS), col0 + start : col0 + start + LANES] = total
        return carry

    lax.fori_loop(0, rows // ROWS, group, 0, unroll=2)


def merged(targets, weights):
    targets = list(targets)
    weights = [list(group) for group in weights]
    count = len(targets)
    for first in range(count):
        for second in range(first + 1, count):
            same = targets[first] == targets[second]
            for group in weights:
                group[first] = group[first] + jnp.where(same, group[second], 0.0)
                group[second] = jnp.where(same, 0.0, group[second])
    return weights


def build_operator(targets, weights, outputs, begin, extent, column):
    count = len(targets)
    tall = 2 * ROWS
    wanted = [jnp.broadcast_to(t - begin, (tall, LANES)).astype(jnp.int16) for t in targets]
    parts = []
    for group in weights:
        for w in group:
            high = w.astype(BF16).astype(F32)
            parts.append(
                (
                    jnp.broadcast_to(high, (tall, LANES)).astype(BF16),
                    jnp.broadcast_to(w - high, (tall, LANES)).astype(BF16),
                )
            )

    def block(step, rows):
        first = pl.multiple_of(step * tall, tall)
        values = [jnp.zeros((tall, LANES), BF16) for _ in range(2 * len(weights))]
        for slot in range(count - 1, -1, -1):
            hit = wanted[slot] == rows
            for g in range(len(weights)):
                high, low = parts[g * count + slot]
                values[2 * g] = jnp.where(hit, high, values[2 * g])
                values[2 * g + 1] = jnp.where(hit, low, values[2 * g + 1])
        for value, ref in zip(values, outputs):
            ref[pl.ds(first, tall), column : column + LANES] = value
        return rows + jnp.int16(tall)

    start = lax.broadcasted_iota(jnp.int32, (tall, LANES), 0).astype(jnp.int16)
    lax.fori_loop(0, extent // tall, block, start, unroll=4)


def chosen_lists(place, lists):
    odd = place[0] & 1
    return lists[pl.ds(1 - odd, 1), :], lists[pl.ds(odd, 1), :]


def send_flow_kernel(place, state, lists, ids, near, far):
    members, width = state.shape[1], lists.shape[1]
    for ref, chosen in zip((near, far), chosen_lists(place, lists)):
        for part in range(2):
            pick_lanes(state.at[1 + part], [chosen], [(ref, part * members, 0)])
        block = jnp.zeros((ref.shape[0] - 2 * members, width), F32)
        row = lax.broadcasted_iota(jnp.int32, block.shape, 0)
        for piece in range(ids.shape[1] // width):
            numbers = ids[:, piece * width : (piece + 1) * width].astype(F32)
            block = jnp.where(row == piece, jnp.broadcast_to(numbers, block.shape), block)
        ref[2 * members :, :] = block


def prepare_kernel(place, state, coef, wet, conn, eh, el, nh, nl, geh, gel, gnh, gnl, totals, partial):
    slots, nodes = conn.shape
    ghosts = geh.shape[0]
    turned = (1 - (place[0] & 1)) * (ghosts // 2)
    for column in range(0, nodes, LANES):
        cut = slice(column, column + LANES)
        targets = []
        for s in range(slots):
            raw = conn[s : s + 1, cut]
            ghost = raw - nodes + turned
            ghost = jnp.where(ghost >= ghosts, ghost - ghosts, ghost)
            targets.append(jnp.where(raw < nodes, raw, nodes + ghost))
        faces = [wet[s : s + 1, cut].astype(F32) for s in range(slots)]
        weights = [[faces[s] * coef[d, s : s + 1, cut] for s in range(slots)] for d in range(2)]
        for d in range(2):
            totals[d : d + 1, cut] = sum(weights[d][1:], weights[d][0])
        weights = merged(targets, weights)
        build_operator(targets, weights, (eh, el, nh, nl), 0, nodes, column)
        build_operator(targets, weights, (geh, gel, gnh, gnl), nodes, ghosts, column)
    partial[...] = (
        product(stacked(state[1]), eh[...], el[...])
        + product(stacked(state[2]), nh[...], nl[...])
        - state[1] * totals[0:1, :]
        - state[2] * totals[1:2, :]
    )


def ghost_flow(near, far, part, members):
    rows = slice(part * members, (part + 1) * members)
    return jnp.concatenate([near[rows, :], far[rows, :]], axis=1)


def level_kernel(place, level, partial, depth, near, far, geh, gel, gnh, gnl, lists, new_level, to_near, to_far):
    members = level.shape[0]
    divergence = (
        partial[...]
        + product(stacked(ghost_flow(near, far, 0, members)), geh[...], gel[...])
        + product(stacked(ghost_flow(near, far, 1, members)), gnh[...], gnl[...])
    )
    new_level[...] = level[...] - DT * depth[...] * divergence
    pick_lanes(new_level, chosen_lists(place, lists), [(to_near, 0, 0), (to_far, 0, 0)])


def last_level_kernel(
    place, level, partial, depth, near, far, geh, gel, gnh, gnl, lists, sampling_high, sampling_low, new_level, to_near, to_far
):
    members, width = level.shape[0], lists.shape[1]
    entries = to_near.shape[1] - width
    level_kernel(place, level, partial, depth, near, far, geh, gel, gnh, gnl, lists, new_level, to_near, to_far)
    seen = product(
        stacked(new_level[...]), sampling_high[:, : 2 * entries], sampling_low[:, : 2 * entries]
    )
    to_near[:, width:] = seen[:, :entries]
    to_far[:, width:] = seen[:, entries:]


def slope_kernel(level, eh, el, nh, nl, totals, east, north):
    stack = stacked(level[...])
    east[...] = product(stack, eh[...], el[...]) - level[...] * totals[0:1, :]
    north[...] = product(stack, nh[...], nl[...]) - level[...] * totals[1:2, :]


def sampling_kernel(
    place, near, far, ids, obs_nodes, obs_weight, obs_value, obs_error, high, low, tables, numbers, scratch, found
):
    members_rows = near.shape[0]
    entries = ids.shape[1]
    width = near.shape[1]
    obs_count = obs_nodes.shape[1]
    base = place[0] * obs_count
    corners = obs_nodes.shape[0]
    precision = 1.0 / (obs_error[...] * obs_error[...])
    scratch[0:corners, :] = obs_nodes[...].astype(F32)
    scratch[corners : 2 * corners, :] = obs_weight[...]
    scratch[2 * corners : 2 * corners + 1, :] = obs_value[...]
    scratch[2 * corners + 1 : 2 * corners + 2, :] = precision
    first = members_rows - ROWS
    for piece in range(entries // width):
        cut = slice(piece * width, (piece + 1) * width)
        numbers[0:1, cut] = near[first + piece : first + piece + 1, :].astype(jnp.int32)
        numbers[1:2, cut] = far[first + piece : first + piece + 1, :].astype(jnp.int32)
    numbers[2:3, :] = ids[...]
    for owner in range(3):
        for start in range(0, entries, LANES):
            index = numbers[owner : owner + 1, start : start + LANES] - base
            own = (index >= 0) & (index < obs_count)
            index = jnp.where(own, index, 0)
            pick_lanes(scratch, [index], [(found, 0, 0)])
            targets = [found[c : c + 1, :].astype(jnp.int32) for c in range(corners)]
            weights = [jnp.where(own, found[corners + c : corners + c + 1, :], 0.0) for c in range(corners)]
            weights = merged(targets, [weights])
            build_operator(targets, weights, (high, low), 0, high.shape[0], owner * entries + start)
            for extra in range(2):
                row = 2 * corners + extra
                tables[2 * owner + extra : 2 * owner + extra + 1, start : start + LANES] = jnp.where(
                    own, found[row : row + 1, :], 0.0
                )


def flow_kernel(
    place, flow, east, north, near, far, geh, gel, gnh, gnl, lists, tables, new_flow, to_near, to_far
):
    members, width = east.shape[0], lists.shape[1]
    stack = stacked(jnp.concatenate([near[...], far[...]], axis=1))
    new_flow[0] = flow[0] - DT * (east[...] + product(stack, geh[...], gel[...]))
    new_flow[1] = flow[1] - DT * (north[...] + product(stack, gnh[...], gnl[...]))
    entries = tables.shape[1]
    chosen = chosen_lists(place, lists)
    for which, ref in enumerate((to_near, to_far)):
        for part in range(2):
            pick_lanes(new_flow.at[part], [chosen[which]], [(ref, part * members, 0)])
        block = jnp.zeros((ref.shape[0] - 2 * members, width), F32)
        row = lax.broadcasted_iota(jnp.int32, block.shape, 0)
        pieces = entries // width
        for extra in range(2):
            for piece in range(pieces):
                values = tables[2 * which + extra : 2 * which + extra + 1, piece * width : (piece + 1) * width]
                block = jnp.where(row == extra * pieces + piece, jnp.broadcast_to(values, block.shape), block)
        ref[2 * members :, :] = block


def divergence_kernel(flow, eh, el, nh, nl, totals, partial):
    partial[...] = (
        product(stacked(flow[0]), eh[...], el[...])
        + product(stacked(flow[1]), nh[...], nl[...])
        - flow[0] * totals[0:1, :]
        - flow[1] * totals[1:2, :]
    )


def last_slope_kernel(level, eh, el, nh, nl, totals, sampling_high, sampling_low, east, north, seen):
    slope_kernel(level, eh, el, nh, nl, totals, east, north)
    entries = seen.shape[1]
    seen[...] = product(
        stacked(level[...]), sampling_high[:, 2 * entries :], sampling_low[:, 2 * entries :]
    )


def inverse_factor(gram):
    size = gram.shape[0]
    row = lax.broadcasted_iota(jnp.int32, (size, size), 0)
    col = lax.broadcasted_iota(jnp.int32, (size, size), 1)
    unit = (row == col).astype(F32)
    table = jnp.concatenate([gram, unit], axis=1)
    blocks = [table[b : b + ROWS, :] for b in range(0, size, ROWS)]
    inner = lax.broadcasted_iota(jnp.int32, (ROWS, 2 * size), 0)
    for pivot in range(size):
        home, spot = divmod(pivot, ROWS)
        line = blocks[home][spot : spot + 1, :]
        scaled = line / line[:, pivot : pivot + 1]
        for b in range(home, len(blocks)):
            factor = blocks[b][:, pivot : pivot + 1]
            change = factor * scaled
            if b == home:
                change = jnp.where(inner > spot, change, 0.0)
            blocks[b] = blocks[b] - change
    table = jnp.concatenate(blocks, axis=0)
    diagonal = jnp.sum(jnp.where(row == col, table[:, :size], 0.0), axis=1, keepdims=True)
    return table[:, size:] * lax.rsqrt(diagonal)


def analysis_kernel(
    length, flow, level, east, north, seen, near, far, tables, early_near, early_far, loc_weight,
    geh, gel, gnh, gnl, out, fields,
):
    members, nodes = level.shape
    entries = seen.shape[1]
    width = near.shape[1] - entries
    stack = stacked(jnp.concatenate([near[:, :width], far[:, :width]], axis=1))
    fields[0] = level[...]
    fields[1] = flow[0] - DT * (east[...] + product(stack, geh[...], gel[...]))
    fields[2] = flow[1] - DT * (north[...] + product(stack, gnh[...], gnl[...]))
    observed = seen[...] + near[:, width:] + far[:, width:]
    obs_mean = jnp.mean(observed, axis=0, keepdims=True)
    anomalies = observed - obs_mean
    pieces = entries // width
    first = early_near.shape[0] - ROWS

    def received(extra):
        rows = [first + extra * pieces + piece for piece in range(pieces)]
        return jnp.concatenate([early_near[r : r + 1, :] + early_far[r : r + 1, :] for r in rows], axis=1)

    value = tables[4:5, :] + received(0)
    precision = tables[5:6, :] + received(1)
    live = lax.broadcasted_iota(jnp.int32, (1, entries), 1) < length[0]
    weight = jnp.where(live, precision * loc_weight[...], 0.0)
    pull = jnp.broadcast_to(weight * (value - obs_mean), (ROWS, entries))
    left = jnp.concatenate([anomalies * weight, pull], axis=0)
    sums = lax.dot_general(left, anomalies, (((1,), (1,)), ((), ())), precision=TOPMOST, preferred_element_type=F32)
    row = lax.broadcasted_iota(jnp.int32, (members, members), 0)
    col = lax.broadcasted_iota(jnp.int32, (members, members), 1)
    gram = sums[:members] + jnp.where(row == col, members - 1.0, 0.0)
    rhs = sums[members : members + 1]
    inverse = inverse_factor(gram)
    halfway = jnp.sum(inverse * rhs, axis=1, keepdims=True)
    mean_w = jnp.sum(inverse * halfway, axis=0, keepdims=True)
    blend = stacked(math.sqrt(members - 1.0) * inverse + mean_w)
    for part in range(3):
        field = fields[part]
        average = jnp.mean(field, axis=0, keepdims=True)
        high, low = halves(field - average)
        out[part] = average + product(blend, high, low)


def call(kernel, outs, args, name, scalars=0, scratch=(), flops=0, final=False, limit=16):
    vmem = pl.BlockSpec(memory_space=pltpu.VMEM)
    in_specs = [pl.BlockSpec(memory_space=pltpu.SMEM)] * scalars + [vmem] * (len(args) - scalars)
    held = sum(math.prod(a.shape) * a.dtype.itemsize for a in list(args) + list(outs))
    if not final:
        outs = [pltpu.VMEM(o.shape, o.dtype) for o in outs]
    args = list(args[:scalars]) + [pltpu.with_memory_space_constraint(a, pltpu.VMEM) for a in args[scalars:]]
    return pl.pallas_call(
        kernel,
        out_shape=outs,
        in_specs=in_specs,
        out_specs=[vmem] * len(outs),
        scratch_shapes=scratch,
        name=name,
        compiler_params=pltpu.CompilerParams(vmem_limit_bytes=limit << 20),
        cost_estimate=pl.CostEstimate(flops=flops, bytes_accessed=held, transcendentals=0),
    )(*args)


def shape(*dims, dtype=F32):
    return jax.ShapeDtypeStruct(dims, dtype)


def exchange(to_near, to_far):
    count = lax.axis_size("mesh")
    pairs = [(i, i ^ 1) for i in range(count)]
    others = [(i, (((i + 1) % count) ^ 1) - 1) for i in range(count)]
    others = [(source, target % count) for source, target in others]
    return lax.ppermute(to_near, "mesh", pairs), lax.ppermute(to_far, "mesh", others)


def local(
    state,
    depth,
    coef,
    wet_faces,
    conn,
    send_list,
    obs_nodes,
    obs_weight,
    obs_value,
    obs_error,
    loc_ids,
    loc_len,
    loc_weight,
):
    members, nodes = state.shape[1:]
    width = send_list.shape[1]
    entries = loc_ids.shape[1]
    ghosts = 2 * width
    assert loc_ids.shape[0] == 1
    depth = depth[None]
    place = lax.axis_index("mesh").astype(jnp.int32)[None]
    work = 8 * members * nodes * nodes

    flow_rows = 2 * members + ROWS
    sent = call(
        send_flow_kernel, [shape(flow_rows, width)] * 2, [place, state, send_list, loc_ids], "send_flow", scalars=1
    )
    from_near, from_far = exchange(*sent)
    big = [shape(nodes, nodes, dtype=BF16)] * 4
    small = [shape(ghosts, nodes, dtype=BF16)] * 4
    made = call(
        prepare_kernel,
        big + small + [shape(2, nodes), shape(members, nodes)],
        [place, state, coef, wet_faces, conn],
        "prepare",
        scalars=1,
        flops=4 * work,
    )
    operators, ghost_operators, totals, partial = made[:4], made[4:8], made[8], made[9]
    level, flow = state[0], state[1:]
    early = (from_near, from_far)
    for step in range(STEPS):
        last = step == STEPS - 1
        columns = width + (entries if last else 0)
        outs = [shape(members, nodes)] + [shape(members, columns)] * 2
        args = [place, level, partial, depth, from_near, from_far, *ghost_operators, send_list]
        if last:
            level, *sent = call(last_level_kernel, outs, args + [sampling_high, sampling_low], "last_level", scalars=1, flops=work)
        else:
            level, *sent = call(level_kernel, outs, args, "level", scalars=1, flops=work)
        from_near, from_far = exchange(*sent)
        slopes = [shape(members, nodes)] * 2
        args = [level, *operators, totals]
        if last:
            east, north, seen = call(
                last_slope_kernel,
                slopes + [shape(members, entries)],
                args + [sampling_high, sampling_low],
                "last_slope",
                flops=2 * work,
            )
            break
        east, north = call(slope_kernel, slopes, args, "slope", flops=2 * work)
        if step == 0:
            sampling_high, sampling_low, tables = call(
                sampling_kernel,
                [shape(nodes, 3 * entries, dtype=BF16)] * 2 + [shape(ROWS, entries)],
                [place, *early, loc_ids, obs_nodes, obs_weight, obs_value[None], obs_error[None]],
                "sampling",
                scalars=1,
                scratch=[
                    pltpu.VMEM((ROWS, entries), jnp.int32),
                    pltpu.VMEM((ROWS, obs_nodes.shape[1]), F32),
                    pltpu.VMEM((ROWS, LANES), F32),
                ],
                flops=work,
            )
        flow, *sent = call(
            flow_kernel,
            [shape(2, members, nodes)] + [shape(flow_rows, width)] * 2,
            [place, flow, east, north, from_near, from_far, *ghost_operators, send_list, tables],
            "flow",
            scalars=1,
            flops=work,
        )
        from_near, from_far = exchange(*sent)
        told = (from_near, from_far)
        (partial,) = call(
            divergence_kernel, [shape(members, nodes)], [flow, *operators, totals], "divergence", flops=2 * work
        )
    (out,) = call(
        analysis_kernel,
        [shape(3, members, nodes)],
        [
            loc_len,
            flow,
            level,
            east,
            north,
            seen,
            from_near,
            from_far,
            tables,
            *told,
            loc_weight,
            *ghost_operators,
        ],
        "analysis",
        scalars=1,
        scratch=[pltpu.VMEM((3, members, nodes), F32)],
        flops=work,
        final=True,
    )
    return out


def solution(mesh):
    spread = ("groups", "mesh")
    in_specs = (
        P(None, None, spread),
        P(spread),
        P(None, None, spread),
        P(None, spread),
        P(None, spread),
        P(None, spread),
        P(None, spread),
        P(None, spread),
        P(spread),
        P(spread),
        P(spread, None),
        P(spread),
        P(spread, None),
    )
    out_specs = P(None, None, spread)
    return jax.shard_map(local, mesh=mesh, in_specs=in_specs, out_specs=out_specs, check_vma=False)
```

```python
import math

import jax
import jax.numpy as jnp
from jax import lax
from jax.experimental import pallas as pl
from jax.experimental.pallas import tpu as pltpu
from jax.sharding import PartitionSpec as P

STEPS = 2
DT = 0.1
LANES = 128
ROWS = 8
F32 = jnp.float32
BF16 = jnp.bfloat16
TOPMOST = lax.Precision.HIGHEST


def halves(value):
    high = value.astype(BF16)
    return high, (value - high.astype(F32)).astype(BF16)


def stacked(value):
    high, low = halves(value)
    return jnp.concatenate([high, low], axis=0)


def product(stack, high, low, first=0, count=None):
    rows = stack.shape[0] // 2
    count = high.shape[0] if count is None else count
    pieces = []
    for tile in range(first, first + count, 2):
        total = 0.0
        for part in (high, low):
            block = jnp.concatenate([part[tile], part[tile + 1]], axis=1)
            total = total + jnp.dot(stack, block, preferred_element_type=F32)
        pieces.append(total[:rows] + total[rows:])
    return jnp.concatenate(pieces, axis=1)


def pick_lanes(sources, indices, targets):
    rows, extent = sources.shape
    plans = []
    for index, target in zip(indices, targets):
        for start in range(0, index.shape[1], LANES):
            wide = jnp.broadcast_to(index[:, start : start + LANES], (ROWS, LANES))
            plans.append((wide & (LANES - 1), wide >> 7, target, start))

    def group(step, carry):
        first = pl.multiple_of(step * ROWS, ROWS)
        for lane, tile, (ref, row0, col0), start in plans:
            total = jnp.zeros((ROWS, LANES), F32)
            for place in range(extent // LANES):
                block = sources[pl.ds(first, ROWS), place * LANES : (place + 1) * LANES]
                found = jnp.take_along_axis(block, lane, axis=1, mode="promise_in_bounds")
                total = jnp.where(tile == place, found, total)
            ref[pl.ds(row0 + first, ROWS), col0 + start : col0 + start + LANES] = total
        return carry

    lax.fori_loop(0, rows // ROWS, group, 0, unroll=4)


def merged(targets, weights):
    targets = list(targets)
    weights = [list(group) for group in weights]
    count = len(targets)
    for first in range(count):
        for second in range(first + 1, count):
            same = targets[first] == targets[second]
            for group in weights:
                group[first] = group[first] + jnp.where(same, group[second], 0.0)
                group[second] = jnp.where(same, 0.0, group[second])
    return weights


def build_operator(targets, weights, outputs, begin, extent, tile):
    count = len(targets)
    tall = 2 * ROWS
    wanted = [jnp.broadcast_to(t - begin, (tall, LANES)).astype(jnp.int16) for t in targets]
    parts = []
    for group in weights:
        for w in group:
            high = w.astype(BF16).astype(F32)
            parts.append(
                (
                    jnp.broadcast_to(high, (tall, LANES)).astype(BF16),
                    jnp.broadcast_to(w - high, (tall, LANES)).astype(BF16),
                )
            )

    def block(step, rows):
        first = pl.multiple_of(step * tall, tall)
        values = [jnp.zeros((tall, LANES), BF16) for _ in range(2 * len(weights))]
        for slot in range(count - 1, -1, -1):
            hit = wanted[slot] == rows
            for g in range(len(weights)):
                high, low = parts[g * count + slot]
                values[2 * g] = jnp.where(hit, high, values[2 * g])
                values[2 * g + 1] = jnp.where(hit, low, values[2 * g + 1])
        for value, ref in zip(values, outputs):
            ref[tile, pl.ds(first, tall), :] = value
        return rows + jnp.int16(tall)

    start = lax.broadcasted_iota(jnp.int32, (tall, LANES), 0).astype(jnp.int16)
    lax.fori_loop(0, extent // tall, block, start, unroll=8)


def chosen_lists(place, lists):
    odd = place[0] & 1
    return lists[pl.ds(1 - odd, 1), :], lists[pl.ds(odd, 1), :]


def live_weight(weight, length):
    entry = lax.broadcasted_iota(jnp.int32, weight.shape, 1)
    return jnp.where(entry < length, weight, 0.0)


def send_flow_kernel(place, length, *refs):
    count = (len(refs) - 3) // 2
    held, (near, far), kept, arrived = refs[:count], refs[count : count + 2], refs[count + 2 : -1], refs[-1]
    state_at, state, lists, ids, weight = held[0], kept[0], kept[1], kept[2], kept[3]
    members, width = state.shape[1], lists.shape[1]
    pairs = [(held[1], lists), (state_at.at[1], state.at[1]), (state_at.at[2], state.at[2])]
    pairs += list(zip(held[2:], kept[2:])) + [(state_at.at[0], state.at[0])]
    copies = [pltpu.make_async_copy(a, b, arrived.at[n]) for n, (a, b) in enumerate(pairs)]
    for copy in copies:
        copy.start()
    copies[0].wait()
    chosen = chosen_lists(place, lists)
    for part in range(2):
        copies[1 + part].wait()
        pick_lanes(state.at[1 + part], chosen, [(near, part * members, 0), (far, part * members, 0)])
    for copy in copies[3:]:
        copy.wait()
    block = jnp.zeros((near.shape[0] - 2 * members, width), F32)
    row = lax.broadcasted_iota(jnp.int32, block.shape, 0)
    pieces = ids.shape[1] // width
    for at, values in enumerate((ids[...].astype(F32), live_weight(weight[...], length[0]))):
        for piece in range(pieces):
            line = values[:, piece * width : (piece + 1) * width]
            block = jnp.where(row == at * pieces + piece, jnp.broadcast_to(line, block.shape), block)
    near[2 * members :, :] = block
    far[2 * members :, :] = block


def prepare_kernel(place, state, coef, wet, conn, eh, el, nh, nl, geh, gel, gnh, gnl, totals, partial):
    slots, nodes = conn.shape
    ghosts = geh.shape[1]
    turned = (1 - (place[0] & 1)) * (ghosts // 2)
    for column in range(0, nodes, LANES):
        cut = slice(column, column + LANES)
        targets = []
        for s in range(slots):
            raw = conn[s : s + 1, cut]
            ghost = raw - nodes + turned
            ghost = jnp.where(ghost >= ghosts, ghost - ghosts, ghost)
            targets.append(jnp.where(raw < nodes, raw, nodes + ghost))
        faces = [wet[s : s + 1, cut].astype(F32) for s in range(slots)]
        weights = [[faces[s] * coef[s, d : d + 1, cut] for s in range(slots)] for d in range(2)]
        for d in range(2):
            totals[d : d + 1, cut] = sum(weights[d][1:], weights[d][0])
        weights = merged(targets, weights)
        build_operator(targets, weights, (eh, el, nh, nl), 0, nodes, column // LANES)
        build_operator(targets, weights, (geh, gel, gnh, gnl), nodes, ghosts, column // LANES)
    partial[...] = (
        product(stacked(state[1]), eh, el)
        + product(stacked(state[2]), nh, nl)
        - state[1] * totals[0:1, :]
        - state[2] * totals[1:2, :]
    )


def ghost_flow(near, far, part, members):
    rows = slice(part * members, (part + 1) * members)
    return jnp.concatenate([near[rows, :], far[rows, :]], axis=1)


def level_kernel(place, held, partial, depth, near, far, geh, gel, gnh, gnl, lists, new_level, to_near, to_far):
    level = held.at[0] if len(held.shape) == 3 else held
    members = level.shape[0]
    divergence = (
        partial[...]
        + product(stacked(ghost_flow(near, far, 0, members)), geh, gel)
        + product(stacked(ghost_flow(near, far, 1, members)), gnh, gnl)
    )
    new_level[...] = level[...] - DT * depth[...] * divergence
    pick_lanes(new_level, chosen_lists(place, lists), [(to_near, 0, 0), (to_far, 0, 0)])


def list_sums(seen, value, weight):
    obs_mean = jnp.mean(seen, axis=0, keepdims=True)
    anomalies = seen - obs_mean
    pull = jnp.broadcast_to(weight * (value - obs_mean), (ROWS, seen.shape[1]))
    left = jnp.concatenate([anomalies * weight, pull], axis=0)
    return lax.dot_general(left, anomalies, (((1,), (1,)), ((), ())), precision=TOPMOST, preferred_element_type=F32)


def last_level_kernel(
    place, level, partial, depth, near, far, geh, gel, gnh, gnl, lists, high, low, tables, new_level, to_near, to_far
):
    members, width = new_level.shape[0], lists.shape[1]
    level_kernel(place, level, partial, depth, near, far, geh, gel, gnh, gnl, lists, new_level, to_near, to_far)
    tiles = high.shape[0] // 3
    stack = stacked(new_level[...])
    for which, ref in enumerate((to_near, to_far)):
        seen = product(stack, high, low, which * tiles, tiles)
        sums = list_sums(seen, tables[2 * which : 2 * which + 1, :], tables[2 * which + 1 : 2 * which + 2, :])
        ref[members:, :width] = jnp.zeros((ROWS, width), F32)
        ref[:, width:] = jnp.concatenate([sums, jnp.zeros((members + ROWS, LANES - members), F32)], axis=1)


def slope_kernel(level, eh, el, nh, nl, totals, east, north):
    stack = stacked(level[...])
    east[...] = product(stack, eh, el) - level[...] * totals[0:1, :]
    north[...] = product(stack, nh, nl) - level[...] * totals[1:2, :]


def sampling_kernel(
    place, length, near, far, ids, weight, obs_nodes, obs_weight, obs_value, obs_error, high, low, tables,
    numbers, strengths, scratch, found,
):
    entries, width = ids.shape[1], near.shape[1]
    corners, obs_count = obs_nodes.shape
    base = place[0] * obs_count
    scratch[0:corners, :] = obs_nodes[...].astype(F32)
    scratch[corners : 2 * corners, :] = obs_weight[...]
    scratch[2 * corners : 2 * corners + 1, :] = obs_value[...]
    scratch[2 * corners + 1 : 2 * corners + 2, :] = 1.0 / (obs_error[...] * obs_error[...])
    first = near.shape[0] - ROWS
    pieces = entries // width
    for piece in range(pieces):
        cut = slice(piece * width, (piece + 1) * width)
        for owner, ref in enumerate((near, far)):
            at = first + piece
            numbers[owner : owner + 1, cut] = ref[at : at + 1, :].astype(jnp.int32)
            strengths[owner : owner + 1, cut] = ref[at + pieces : at + pieces + 1, :]
    numbers[2:3, :] = ids[...]
    strengths[2:3, :] = live_weight(weight[...], length[0])
    tiles = entries // LANES
    places = [(owner, tile) for owner in range(3) for tile in range(tiles)]
    kept = {}
    for owner, tile in places:
        index = numbers[owner : owner + 1, tile * LANES : (tile + 1) * LANES] - base
        own = (index >= 0) & (index < obs_count)
        kept[owner, tile] = own, jnp.where(own, index, 0)
    pick_lanes(
        scratch,
        [kept[spot][1] for spot in places],
        [(found, 0, (owner * tiles + tile) * LANES) for owner, tile in places],
    )
    for owner, tile in places:
        at = owner * tiles + tile
        own = kept[owner, tile][0]
        here = found[:, at * LANES : (at + 1) * LANES]
        targets = [here[c : c + 1, :].astype(jnp.int32) for c in range(corners)]
        shares = [jnp.where(own, here[corners + c : corners + c + 1, :], 0.0) for c in range(corners)]
        shares = merged(targets, [shares])
        build_operator(targets, shares, (high, low), 0, high.shape[1], at)
        cut = slice(tile * LANES, (tile + 1) * LANES)
        force = here[2 * corners + 1 : 2 * corners + 2, :] * strengths[owner : owner + 1, cut]
        tables[2 * owner : 2 * owner + 1, cut] = here[2 * corners : 2 * corners + 1, :]
        tables[2 * owner + 1 : 2 * owner + 2, cut] = jnp.where(own, force, 0.0)


def flow_kernel(place, flow, east, north, near, far, geh, gel, gnh, gnl, lists, new_flow, to_near, to_far):
    members = east.shape[0]
    stack = stacked(jnp.concatenate([near[...], far[...]], axis=1))
    chosen = chosen_lists(place, lists)
    first = flow.shape[0] - 2
    new_flow[0] = flow[first] - DT * (east[...] + product(stack, geh, gel))
    new_flow[1] = flow[first + 1] - DT * (north[...] + product(stack, gnh, gnl))
    for part in range(2):
        pick_lanes(new_flow.at[part], chosen, [(to_near, part * members, 0), (to_far, part * members, 0)])


def divergence_kernel(flow, eh, el, nh, nl, totals, partial):
    partial[...] = (
        product(stacked(flow[0]), eh, el)
        + product(stacked(flow[1]), nh, nl)
        - flow[0] * totals[0:1, :]
        - flow[1] * totals[1:2, :]
    )


def last_slope_kernel(level, eh, el, nh, nl, totals, high, low, tables, east, north, sums):
    slope_kernel(level, eh, el, nh, nl, totals, east, north)
    tiles = high.shape[0] // 3
    seen = product(stacked(level[...]), high, low, 2 * tiles, tiles)
    sums[...] = list_sums(seen, tables[4:5, :], tables[5:6, :])


def pair_inverse(a, b, c):
    r = 1.0 / (a * c - b * b)
    return c * r, -(b * r), a * r


def pair_rows(a, b, c, first, second):
    m = b / a
    return first * lax.rsqrt(a), (second - m * first) * lax.rsqrt(c - m * b)


def inverse_factor(gram):
    size = gram.shape[0]
    wide = (ROWS, 2 * size)
    row = lax.broadcasted_iota(jnp.int32, (size, size), 0)
    col = lax.broadcasted_iota(jnp.int32, (size, size), 1)
    table = jnp.concatenate([gram, (row == col).astype(F32)], axis=1)
    blocks = [table[b : b + ROWS, :] for b in range(0, size, ROWS)]
    inner = lax.broadcasted_iota(jnp.int32, wide, 0)

    def spread(value):
        return jnp.broadcast_to(value, wide)

    done = []
    for home in range(len(blocks)):
        result = jnp.zeros(wide, F32)
        for spot in range(0, ROWS, 4):
            pivot = home * ROWS + spot
            lines = [spread(blocks[home][spot + i : spot + i + 1, :]) for i in range(4)]
            columns = [spread(blocks[home][:, pivot + i : pivot + i + 1]) for i in range(4)]

            def entry(i, j):
                return spread(columns[j][spot + i : spot + i + 1, :])

            head = entry(0, 0), entry(1, 0), entry(1, 1)
            p = pair_inverse(*head)
            b = [[entry(2 + i, j) for j in range(2)] for i in range(2)]
            t = [[b[i][0] * p[0] + b[i][1] * p[1], b[i][0] * p[1] + b[i][1] * p[2]] for i in range(2)]
            tail = (
                entry(2, 2) - (t[0][0] * b[0][0] + t[0][1] * b[0][1]),
                entry(3, 2) - (t[1][0] * b[0][0] + t[1][1] * b[0][1]),
                entry(3, 3) - (t[1][0] * b[1][0] + t[1][1] * b[1][1]),
            )
            rest = [lines[2 + i] - (t[i][0] * lines[0] + t[i][1] * lines[1]) for i in range(2)]
            q = pair_inverse(*tail)
            z2 = q[0] * rest[0] + q[1] * rest[1]
            z3 = q[1] * rest[0] + q[2] * rest[1]
            z0 = (p[0] * lines[0] + p[1] * lines[1]) - (t[0][0] * z2 + t[1][0] * z3)
            z1 = (p[1] * lines[0] + p[2] * lines[1]) - (t[0][1] * z2 + t[1][1] * z3)
            final = pair_rows(*head, lines[0], lines[1]) + pair_rows(*tail, rest[0], rest[1])
            for i, value in enumerate(final):
                result = jnp.where(inner == spot + i, value, result)
            for place in range(home, len(blocks)):
                factors = columns
                if place > home:
                    factors = [spread(blocks[place][:, pivot + i : pivot + i + 1]) for i in range(4)]
                elif spot + 4 == ROWS:
                    continue
                change = (factors[2] * z2 + factors[3] * z3) + (factors[0] * z0 + factors[1] * z1)
                if place == home:
                    change = jnp.where(inner >= spot + 4, change, 0.0)
                blocks[place] = blocks[place] - change
        done.append(result)
    return jnp.concatenate(done, axis=0)[:, size:]


def analysis_kernel(flow, level, east, north, sums, near, far, geh, gel, gnh, gnl, out, fields):
    members = level.shape[0]
    width = near.shape[1] - LANES
    total = sums[...] + near[:, width : width + members] + far[:, width : width + members]
    row = lax.broadcasted_iota(jnp.int32, (members, members), 0)
    col = lax.broadcasted_iota(jnp.int32, (members, members), 1)
    gram = total[:members] + jnp.where(row == col, members - 1.0, 0.0)
    rhs = total[members : members + 1]
    inverse = inverse_factor(gram)
    stack = stacked(jnp.concatenate([near[:members, :width], far[:members, :width]], axis=1))
    fields[0] = level[...]
    fields[1] = flow[0] - DT * (east[...] + product(stack, geh, gel))
    fields[2] = flow[1] - DT * (north[...] + product(stack, gnh, gnl))
    halfway = jnp.sum(inverse * rhs, axis=1, keepdims=True)
    mean_w = jnp.sum(inverse * halfway, axis=0, keepdims=True)
    blend = stacked(math.sqrt(members - 1.0) * inverse + mean_w)
    for part in range(3):
        field = fields[part]
        average = jnp.mean(field, axis=0, keepdims=True)
        high, low = halves(field - average)
        moved = jnp.dot(blend, high, preferred_element_type=F32) + jnp.dot(blend, low, preferred_element_type=F32)
        out[part] = average + moved[:members] + moved[members:]


def call(kernel, outs, args, scalars=0, scratch=(), flops=0, final=False, limit=16, raw=False):
    vmem = pl.BlockSpec(memory_space=pltpu.VMEM)
    in_specs = [pl.BlockSpec(memory_space=pltpu.SMEM)] * scalars + [pl.BlockSpec(memory_space=pltpu.HBM) if raw else vmem] * (len(args) - scalars)
    held = sum(math.prod(a.shape) * a.dtype.itemsize for a in list(args) + list(outs))
    if not final:
        outs = [pltpu.VMEM(o.shape, o.dtype) for o in outs]
    space = pltpu.HBM if raw else pltpu.VMEM
    args = list(args[:scalars]) + [pltpu.with_memory_space_constraint(a, space) for a in args[scalars:]]
    return pl.pallas_call(
        kernel,
        out_shape=outs,
        in_specs=in_specs,
        out_specs=[vmem] * len(outs),
        scratch_shapes=scratch,
        compiler_params=pltpu.CompilerParams(vmem_limit_bytes=limit << 20),
        cost_estimate=pl.CostEstimate(flops=flops, bytes_accessed=held, transcendentals=0),
    )(*args)


def shape(*dims, dtype=F32):
    return jax.ShapeDtypeStruct(dims, dtype)


def exchange(to_near, to_far):
    count = lax.axis_size("mesh")
    pairs = [(i, i ^ 1) for i in range(count)]
    others = [(i, (((i + 1) % count) ^ 1) - 1) for i in range(count)]
    others = [(source, target % count) for source, target in others]
    from_far = lax.ppermute(to_far, "mesh", others)
    from_near = lax.ppermute(to_near, "mesh", pairs)
    return from_near, from_far


def local(
    state,
    depth,
    coef,
    wet_faces,
    conn,
    send_list,
    obs_nodes,
    obs_weight,
    obs_value,
    obs_error,
    loc_ids,
    loc_len,
    loc_weight,
):
    members, nodes = state.shape[1:]
    width = send_list.shape[1]
    entries = loc_ids.shape[1]
    ghosts = 2 * width
    tiles = nodes // LANES
    assert loc_ids.shape[0] == 1
    depth = depth[None]
    place = lax.axis_index("mesh").astype(jnp.int32)[None]
    work = 8 * members * nodes * nodes

    brought = [state, send_list, loc_ids, loc_weight, depth, jnp.swapaxes(coef, 0, 1), wet_faces, conn]
    brought += [obs_nodes, obs_weight, obs_value[None], obs_error[None]]
    near, far, *brought = call(
        send_flow_kernel,
        [shape(2 * members + ROWS, width)] * 2 + [shape(*a.shape, dtype=a.dtype) for a in brought],
        [place, loc_len, *brought],
        scalars=2,
        scratch=[pltpu.SemaphoreType.DMA((len(brought) + 2,))],
        raw=True,
    )
    sent = [near, far]
    state, send_list, loc_ids, loc_weight, depth, coef, wet_faces, conn = brought[:8]
    obs_nodes, obs_weight, obs_value, obs_error = brought[8:]
    from_near, from_far = exchange(*sent)
    big = [shape(tiles, nodes, LANES, dtype=BF16)] * 4
    small = [shape(tiles, ghosts, LANES, dtype=BF16)] * 4
    made = call(
        prepare_kernel,
        big + small + [shape(2, nodes), shape(members, nodes)],
        [place, state, coef, wet_faces, conn],
        scalars=1,
        flops=4 * work,
    )
    operators, ghost_operators, totals, partial = made[:4], made[4:8], made[8], made[9]
    level = flow = state
    early = from_near, from_far
    for step in range(STEPS):
        last = step == STEPS - 1
        args = [place, level, partial, depth, from_near, from_far, *ghost_operators, send_list]
        kernel, extra, payload = level_kernel, [], shape(members, width)
        if last:
            kernel, extra, payload = last_level_kernel, list(sampling), shape(members + ROWS, width + LANES)
        level, *sent = call(kernel, [shape(members, nodes), payload, payload], args + extra, scalars=1, flops=work)
        from_near, from_far = exchange(*sent)
        slopes = [shape(members, nodes)] * 2
        args = [level, *operators, totals]
        if last:
            east, north, sums = call(
                last_slope_kernel, slopes + [shape(members + ROWS, members)], args + list(sampling), flops=2 * work
            )
            break
        east, north = call(slope_kernel, slopes, args, flops=2 * work)
        flow, *sent = call(
            flow_kernel,
            [shape(2, members, nodes)] + [shape(2 * members, width)] * 2,
            [place, flow, east, north, from_near, from_far, *ghost_operators, send_list],
            scalars=1,
            flops=work,
        )
        early, sent[0] = lax.optimization_barrier((early, sent[0]))
        from_near, from_far = exchange(*sent)
        (partial,) = call(divergence_kernel, [shape(members, nodes)], [flow, *operators, totals], flops=2 * work)
        sampling = call(
            sampling_kernel,
            [shape(3 * entries // LANES, nodes, LANES, dtype=BF16)] * 2 + [shape(ROWS, entries)],
            [place, loc_len, *early, loc_ids, loc_weight, obs_nodes, obs_weight, obs_value, obs_error],
            scalars=2,
            scratch=[
                pltpu.VMEM((ROWS, entries), jnp.int32),
                pltpu.VMEM((ROWS, entries), F32),
                pltpu.VMEM((ROWS, obs_nodes.shape[1]), F32),
                pltpu.VMEM((ROWS, 3 * entries), F32),
            ],
            flops=work,
        )
    (out,) = call(
        analysis_kernel,
        [shape(3, members, nodes)],
        [flow, level, east, north, sums, from_near, from_far, *ghost_operators],
        scratch=[pltpu.VMEM((3, members, nodes), F32)],
        flops=work,
        final=True,
    )
    return out


def solution(mesh):
    spread = ("groups", "mesh")
    in_specs = (
        P(None, None, spread),
        P(spread),
        P(None, None, spread),
        P(None, spread),
        P(None, spread),
        P(None, spread),
        P(None, spread),
        P(None, spread),
        P(spread),
        P(spread),
        P(spread, None),
        P(spread),
        P(spread, None),
    )
    out_specs = P(None, None, spread)
    return jax.shard_map(local, mesh=mesh, in_specs=in_specs, out_specs=out_specs, check_vma=False)
```

```python
import functools
import math

import jax
import jax.numpy as jnp
from jax import lax
from jax.experimental import pallas as pl
from jax.experimental.pallas import tpu as pltpu
from jax.sharding import PartitionSpec as P

DT = 0.1
LANES = 128
ROWS = 8
F32 = jnp.float32
BF16 = jnp.bfloat16


def halves(value):
    high = value.astype(BF16)
    return high, (value - high.astype(F32)).astype(BF16)


def stacked(value):
    high, low = halves(value)
    return jnp.concatenate([high, low], axis=0)


def product(stack, high, low, first=0, count=None):
    rows = stack.shape[0] // 2
    count = high.shape[0] if count is None else count
    pieces = []
    for tile in range(first, first + count, 2):
        total = 0.0
        for part in (high, low):
            block = jnp.concatenate([part[tile], part[tile + 1]], axis=1)
            total = total + jnp.dot(stack, block, preferred_element_type=F32)
        pieces.append(total[:rows] + total[rows:])
    return jnp.concatenate(pieces, axis=1)


def pick_lanes(sources, indices, targets):
    rows, extent = sources.shape
    plans = []
    for index, target in zip(indices, targets):
        for start in range(0, index.shape[1], LANES):
            wide = jnp.broadcast_to(index[:, start : start + LANES], (ROWS, LANES))
            plans.append((wide & (LANES - 1), wide >> 7, target, start))

    def group(step, carry):
        first = pl.multiple_of(step * ROWS, ROWS)
        for lane, tile, (ref, row0, col0), start in plans:
            total = jnp.zeros((ROWS, LANES), F32)
            for place in range(extent // LANES):
                block = sources[pl.ds(first, ROWS), place * LANES : (place + 1) * LANES]
                found = jnp.take_along_axis(block, lane, axis=1, mode="promise_in_bounds")
                total = jnp.where(tile == place, found, total)
            ref[pl.ds(row0 + first, ROWS), col0 + start : col0 + start + LANES] = total
        return carry

    lax.fori_loop(0, rows // ROWS, group, 0, unroll=4)


def merged(targets, weights):
    targets = list(targets)
    weights = [list(group) for group in weights]
    count = len(targets)
    for first in range(count):
        for second in range(first + 1, count):
            same = targets[first] == targets[second]
            for group in weights:
                group[first] = group[first] + jnp.where(same, group[second], 0.0)
                group[second] = jnp.where(same, 0.0, group[second])
    return weights


def build_operator(targets, weights, outputs, begin, extent, tile):
    count = len(targets)
    tall = 2 * ROWS
    wanted = [jnp.broadcast_to(t - begin, (tall, LANES)).astype(jnp.int16) for t in targets]
    parts = []
    for group in weights:
        for w in group:
            high = w.astype(BF16).astype(F32)
            parts.append(
                (
                    jnp.broadcast_to(high, (tall, LANES)).astype(BF16),
                    jnp.broadcast_to(w - high, (tall, LANES)).astype(BF16),
                )
            )

    def block(step, rows):
        first = pl.multiple_of(step * tall, tall)
        values = [jnp.zeros((tall, LANES), BF16) for _ in range(2 * len(weights))]
        for slot in range(count - 1, -1, -1):
            hit = wanted[slot] == rows
            for g in range(len(weights)):
                high, low = parts[g * count + slot]
                values[2 * g] = jnp.where(hit, high, values[2 * g])
                values[2 * g + 1] = jnp.where(hit, low, values[2 * g + 1])
        for value, ref in zip(values, outputs):
            ref[tile, pl.ds(first, tall), :] = value
        return rows + jnp.int16(tall)

    start = lax.broadcasted_iota(jnp.int32, (tall, LANES), 0).astype(jnp.int16)
    lax.fori_loop(0, extent // tall, block, start, unroll=8)


def chosen_lists(place, lists):
    odd = place[0] & 1
    return lists[pl.ds(1 - odd, 1), :], lists[pl.ds(odd, 1), :]


def live_weight(weight, length):
    entry = lax.broadcasted_iota(jnp.int32, weight.shape, 1)
    return jnp.where(entry < length, weight, 0.0)


def send_flow_kernel(place, length, *refs):
    count = (len(refs) - 3) // 2
    held, (near, far), kept, arrived = refs[:count], refs[count : count + 2], refs[count + 2 : -1], refs[-1]
    state_at, state, lists, ids, weight = held[0], kept[0], kept[1], kept[2], kept[3]
    members, width = state.shape[1], lists.shape[1]
    pairs = [(held[1], lists), (state_at.at[1], state.at[1]), (state_at.at[2], state.at[2])]
    pairs += list(zip(held[2:], kept[2:])) + [(state_at.at[0], state.at[0])]
    copies = [pltpu.make_async_copy(a, b, arrived.at[n]) for n, (a, b) in enumerate(pairs)]
    for copy in copies:
        copy.start()
    copies[0].wait()
    chosen = chosen_lists(place, lists)
    for part in range(2):
        copies[1 + part].wait()
        pick_lanes(state.at[1 + part], chosen, [(near, part * members, 0), (far, part * members, 0)])
    for copy in copies[3:]:
        copy.wait()
    block = jnp.zeros((near.shape[0] - 2 * members, width), F32)
    row = lax.broadcasted_iota(jnp.int32, block.shape, 0)
    pieces = ids.shape[1] // width
    for at, values in enumerate((ids[...].astype(F32), live_weight(weight[...], length[0]))):
        for piece in range(pieces):
            line = values[:, piece * width : (piece + 1) * width]
            block = jnp.where(row == at * pieces + piece, jnp.broadcast_to(line, block.shape), block)
    near[2 * members :, :] = block
    far[2 * members :, :] = block


def prepare_kernel(place, coef, wet, conn, eh, el, nh, nl, geh, gel, gnh, gnl, totals):
    slots, nodes = conn.shape
    ghosts = geh.shape[1]
    turned = (1 - (place[0] & 1)) * (ghosts // 2)
    for column in range(0, nodes, LANES):
        cut = slice(column, column + LANES)
        targets = []
        for s in range(slots):
            raw = conn[s : s + 1, cut]
            ghost = raw - nodes + turned
            ghost = jnp.where(ghost >= ghosts, ghost - ghosts, ghost)
            targets.append(jnp.where(raw < nodes, raw, nodes + ghost))
        faces = [wet[s : s + 1, cut].astype(F32) for s in range(slots)]
        weights = [[faces[s] * coef[s, d : d + 1, cut] for s in range(slots)] for d in range(2)]
        for d in range(2):
            totals[d : d + 1, cut] = sum(weights[d][1:], weights[d][0])
        weights = merged(targets, weights)
        build_operator(targets, weights, (eh, el, nh, nl), 0, nodes, column // LANES)
        build_operator(targets, weights, (geh, gel, gnh, gnl), nodes, ghosts, column // LANES)


def ghost_flow(near, far, part, members):
    rows = slice(part * members, (part + 1) * members)
    return jnp.concatenate([near[rows, :], far[rows, :]], axis=1)


def stepped_level(held, partial, depth, near, far, geh, gel, gnh, gnl):
    level = held.at[0] if len(held.shape) == 3 else held
    members = level.shape[0]
    divergence = (
        partial[...]
        + product(stacked(ghost_flow(near, far, 0, members)), geh, gel)
        + product(stacked(ghost_flow(near, far, 1, members)), gnh, gnl)
    )
    return level[...] - DT * depth[...] * divergence


def level_kernel(place, held, partial, depth, near, far, geh, gel, gnh, gnl, lists, new_level, to_near, to_far):
    new_level[...] = stepped_level(held, partial, depth, near, far, geh, gel, gnh, gnl)
    pick_lanes(new_level, chosen_lists(place, lists), [(to_near, 0, 0), (to_far, 0, 0)])


def thirds(value):
    high, rest = halves(value)
    middle = rest
    low = (value - high.astype(F32) - middle.astype(F32)).astype(BF16)
    return high, middle, low


def row_products(left, right):
    rows = left.shape[0]
    ours, theirs = thirds(left), thirds(right)
    total = 0.0
    for skip, part in enumerate(theirs):
        block = jnp.concatenate(ours[: 3 - skip], axis=0)
        found = lax.dot_general(block, part, (((1,), (1,)), ((), ())), preferred_element_type=F32)
        sums = [found[at * rows : (at + 1) * rows] for at in range(3 - skip)]
        while len(sums) > 1:
            sums[-2:] = [sums[-2] + sums[-1]]
        total = sums[0] + total
    return total


def list_sums(seen, value, weight):
    obs_mean = jnp.mean(seen, axis=0, keepdims=True)
    anomalies = seen - obs_mean
    pull = jnp.broadcast_to(weight * (value - obs_mean), (ROWS, seen.shape[1]))
    left = jnp.concatenate([anomalies * weight, pull], axis=0)
    return row_products(left, anomalies)


def neighbour_payload(which, place, level, lists, high, low, tables, ref):
    members, width = level.shape[0], lists.shape[1]
    tiles = high.shape[0] // 2
    pick_lanes(level, [chosen_lists(place, lists)[which]], [(ref, 0, 0)])
    seen = product(stacked(level[...]), high, low, which * tiles, tiles)
    sums = list_sums(seen, tables[2 * which : 2 * which + 1, :], tables[2 * which + 1 : 2 * which + 2, :])
    ref[members:, :width] = jnp.zeros((ROWS, width), F32)
    ref[:, width:] = jnp.concatenate([sums, jnp.zeros((members + ROWS, LANES - members), F32)], axis=1)


def last_level_kernel(
    place, held, partial, depth, near, far, geh, gel, gnh, gnl, lists, high, low, tables, new_level, to_far
):
    new_level[...] = stepped_level(held, partial, depth, near, far, geh, gel, gnh, gnl)
    neighbour_payload(1, place, new_level, lists, high, low, tables, to_far)


def near_sums_kernel(place, level, lists, high, low, tables, to_near):
    neighbour_payload(0, place, level, lists, high, low, tables, to_near)


def slope_kernel(level, eh, el, nh, nl, totals, east, north):
    stack = stacked(level[...])
    east[...] = product(stack, eh, el) - level[...] * totals[0:1, :]
    north[...] = product(stack, nh, nl) - level[...] * totals[1:2, :]


def sampling_kernel(
    place, length, near, far, ids, weight, obs_nodes, obs_weight, obs_value, obs_error, high, low, tables, found,
    numbers, strengths, scratch,
):
    entries, width = ids.shape[1], near.shape[1]
    corners, obs_count = obs_nodes.shape
    base = place[0] * obs_count
    scratch[0:corners, :] = obs_nodes[...].astype(F32)
    scratch[corners : 2 * corners, :] = obs_weight[...]
    scratch[2 * corners : 2 * corners + 1, :] = obs_value[...]
    scratch[2 * corners + 1 : 2 * corners + 2, :] = 1.0 / (obs_error[...] * obs_error[...])
    first = near.shape[0] - ROWS
    pieces = entries // width
    for piece in range(pieces):
        cut = slice(piece * width, (piece + 1) * width)
        for owner, ref in enumerate((near, far)):
            at = first + piece
            numbers[owner : owner + 1, cut] = ref[at : at + 1, :].astype(jnp.int32)
            strengths[owner : owner + 1, cut] = ref[at + pieces : at + pieces + 1, :]
    numbers[2:3, :] = ids[...]
    strengths[2:3, :] = live_weight(weight[...], length[0])
    tiles = entries // LANES
    places = [(owner, tile) for owner in range(3) for tile in range(tiles)]
    kept = {}
    for owner, tile in places:
        index = numbers[owner : owner + 1, tile * LANES : (tile + 1) * LANES] - base
        own = (index >= 0) & (index < obs_count)
        kept[owner, tile] = own, jnp.where(own, index, 0)
    pick_lanes(
        scratch,
        [kept[spot][1] for spot in places],
        [(found, 0, (owner * tiles + tile) * LANES) for owner, tile in places],
    )
    for owner, tile in places:
        at = slice((owner * tiles + tile) * LANES, (owner * tiles + tile + 1) * LANES)
        own = kept[owner, tile][0]
        cut = slice(tile * LANES, (tile + 1) * LANES)
        found[corners : 2 * corners, at] = jnp.where(own, found[corners : 2 * corners, at], 0.0)
        force = found[2 * corners + 1 : 2 * corners + 2, at] * strengths[owner : owner + 1, cut]
        tables[2 * owner : 2 * owner + 1, cut] = found[2 * corners : 2 * corners + 1, at]
        tables[2 * owner + 1 : 2 * owner + 2, cut] = jnp.where(own, force, 0.0)
    corner_operator(found, 2 * tiles, corners, high, low)


def corner_operator(found, first, corners, high, low):
    for tile in range(high.shape[0]):
        here = found[:, (first + tile) * LANES : (first + tile + 1) * LANES]
        targets = [here[c : c + 1, :].astype(jnp.int32) for c in range(corners)]
        shares = [here[corners + c : corners + c + 1, :] for c in range(corners)]
        build_operator(targets, merged(targets, [shares]), (high, low), 0, high.shape[1], tile)


def others_kernel(corners, found, high, low):
    corner_operator(found, 0, corners, high, low)


def flow_kernel(place, flow, east, north, near, far, geh, gel, gnh, gnl, lists, new_flow, to_near, to_far):
    members = east.shape[0]
    stack = stacked(jnp.concatenate([near[...], far[...]], axis=1))
    chosen = chosen_lists(place, lists)
    first = flow.shape[0] - 2
    new_flow[0] = flow[first] - DT * (east[...] + product(stack, geh, gel))
    new_flow[1] = flow[first + 1] - DT * (north[...] + product(stack, gnh, gnl))
    for part in range(2):
        pick_lanes(new_flow.at[part], chosen, [(to_near, part * members, 0), (to_far, part * members, 0)])


def divergence_kernel(flow, eh, el, nh, nl, totals, partial):
    first = flow.shape[0] - 2
    east, north = flow[first], flow[first + 1]
    partial[...] = (
        product(stacked(east), eh, el)
        + product(stacked(north), nh, nl)
        - east * totals[0:1, :]
        - north * totals[1:2, :]
    )


def own_sums_kernel(level, high, low, tables, sums):
    sums[...] = list_sums(product(stacked(level[...]), high, low), tables[4:5, :], tables[5:6, :])


def pair_inverse(a, b, c):
    r = 1.0 / (a * c - b * b)
    return c * r, -(b * r), a * r


def pair_rows(a, b, c, first, second):
    m = b / a
    return first * lax.rsqrt(a), (second - m * first) * lax.rsqrt(c - m * b)


def inverse_factor(gram, beside):
    size = gram.shape[0]
    wide = (ROWS, 2 * size)
    row = lax.broadcasted_iota(jnp.int32, (size, size), 0)
    col = lax.broadcasted_iota(jnp.int32, (size, size), 1)
    table = jnp.concatenate([gram, (row == col).astype(F32)], axis=1)
    blocks = [table[b : b + ROWS, :] for b in range(0, size, ROWS)]
    inner = lax.broadcasted_iota(jnp.int32, wide, 0)

    def spread(value):
        return jnp.broadcast_to(value, wide)

    done = []
    for home in range(len(blocks)):
        result = jnp.zeros(wide, F32)
        for spot in range(0, ROWS, 4):
            pivot = home * ROWS + spot
            lines = [spread(blocks[home][spot + i : spot + i + 1, :]) for i in range(4)]
            columns = [spread(blocks[home][:, pivot + i : pivot + i + 1]) for i in range(4)]

            def entry(i, j):
                return spread(columns[j][spot + i : spot + i + 1, :])

            head = entry(0, 0), entry(1, 0), entry(1, 1)
            p = pair_inverse(*head)
            b = [[entry(2 + i, j) for j in range(2)] for i in range(2)]
            t = [[b[i][0] * p[0] + b[i][1] * p[1], b[i][0] * p[1] + b[i][1] * p[2]] for i in range(2)]
            tail = (
                entry(2, 2) - (t[0][0] * b[0][0] + t[0][1] * b[0][1]),
                entry(3, 2) - (t[1][0] * b[0][0] + t[1][1] * b[0][1]),
                entry(3, 3) - (t[1][0] * b[1][0] + t[1][1] * b[1][1]),
            )
            rest = [lines[2 + i] - (t[i][0] * lines[0] + t[i][1] * lines[1]) for i in range(2)]
            q = pair_inverse(*tail)
            z2 = q[0] * rest[0] + q[1] * rest[1]
            z3 = q[1] * rest[0] + q[2] * rest[1]
            z0 = (p[0] * lines[0] + p[1] * lines[1]) - (t[0][0] * z2 + t[1][0] * z3)
            z1 = (p[1] * lines[0] + p[2] * lines[1]) - (t[0][1] * z2 + t[1][1] * z3)
            final = pair_rows(*head, lines[0], lines[1]) + pair_rows(*tail, rest[0], rest[1])
            for i, value in enumerate(final):
                result = jnp.where(inner == spot + i, value, result)
            for place in range(home, len(blocks)):
                factors = columns
                if place > home:
                    factors = [spread(blocks[place][:, pivot + i : pivot + i + 1]) for i in range(4)]
                elif spot + 4 == ROWS:
                    continue
                change = (factors[2] * z2 + factors[3] * z3) + (factors[0] * z0 + factors[1] * z1)
                if place == home:
                    change = jnp.where(inner >= spot + 4, change, 0.0)
                blocks[place] = blocks[place] - change
            beside()
        done.append(result)
    return jnp.concatenate(done, axis=0)[:, size:]


def analysis_kernel(
    flow, level, east, north, sums, near, far, geh, gel, gnh, gnl, out, result, moved, averages, sent
):
    members, nodes = level.shape
    width = near.shape[1] - LANES
    total = sums[...] + near[:, width : width + members] + far[:, width : width + members]
    row = lax.broadcasted_iota(jnp.int32, (members, members), 0)
    col = lax.broadcasted_iota(jnp.int32, (members, members), 1)
    gram = total[:members] + jnp.where(row == col, members - 1.0, 0.0)
    rhs = total[members : members + 1]
    stack = stacked(jnp.concatenate([near[:members, :width], far[:members, :width]], axis=1))
    operators = ((geh, gel), (gnh, gnl))

    def piece(part, tile):
        cut = slice(tile * LANES, (tile + 2) * LANES)
        if part == 0:
            field = level[:, cut]
        else:
            slope = (east, north)[part - 1][:, cut] + product(stack, *operators[part - 1], tile, 2)
            field = flow[part - 1, :, cut] - DT * slope
        average = jnp.mean(field, axis=0, keepdims=True)
        moved[part, :, cut] = stacked(field - average)
        averages[part : part + 1, cut] = average

    pieces = [(part, tile) for part in (1, 2, 0) for tile in range(0, nodes // LANES, 2)]

    def beside():
        if pieces:
            piece(*pieces.pop(0))

    inverse = inverse_factor(gram, beside)
    while pieces:
        beside()
    halfway = jnp.sum(inverse * rhs, axis=1, keepdims=True)
    mean_w = jnp.sum(inverse * halfway, axis=0, keepdims=True)
    blend = math.sqrt(members - 1.0) * inverse + mean_w
    blend = stacked(jnp.concatenate([blend, blend], axis=1))
    copies = []
    for part in range(3):
        change = jnp.dot(blend, moved[part], preferred_element_type=F32)
        result[part] = averages[part : part + 1, :] + (change[:members] + change[members:])
        copies.append(pltpu.make_async_copy(result.at[part], out.at[part], sent.at[part]))
        copies[-1].start()
    for copy in copies:
        copy.wait()


def call(kernel, outs, args, scalars=0, scratch=(), flops=0, final=False, limit=16, raw=False):
    vmem = pl.BlockSpec(memory_space=pltpu.VMEM)
    in_specs = [pl.BlockSpec(memory_space=pltpu.SMEM)] * scalars + [pl.BlockSpec(memory_space=pltpu.HBM) if raw else vmem] * (len(args) - scalars)
    held = sum(math.prod(a.shape) * a.dtype.itemsize for a in list(args) + list(outs))
    if not final:
        outs = [pltpu.VMEM(o.shape, o.dtype) for o in outs]
    space = pltpu.HBM if raw else pltpu.VMEM
    args = list(args[:scalars]) + [pltpu.with_memory_space_constraint(a, space) for a in args[scalars:]]
    return pl.pallas_call(
        kernel,
        out_shape=outs,
        in_specs=in_specs,
        out_specs=[pl.BlockSpec(memory_space=pltpu.HBM) if final else vmem] * len(outs),
        scratch_shapes=scratch,
        compiler_params=pltpu.CompilerParams(vmem_limit_bytes=limit << 20),
        cost_estimate=pl.CostEstimate(flops=flops, bytes_accessed=held, transcendentals=0),
    )(*args)


def shape(*dims, dtype=F32):
    return jax.ShapeDtypeStruct(dims, dtype)


def to_partner(value):
    pairs = [(i, i ^ 1) for i in range(lax.axis_size("mesh"))]
    return lax.ppermute(value, "mesh", pairs)


def to_other(value):
    count = lax.axis_size("mesh")
    others = [(i, ((i + 1) ^ 1) - 1) for i in range(1, count - 1)]
    return lax.ppermute(value, "mesh", others)


def local(
    state,
    depth,
    coef,
    wet_faces,
    conn,
    send_list,
    obs_nodes,
    obs_weight,
    obs_value,
    obs_error,
    loc_ids,
    loc_len,
    loc_weight,
):
    members, nodes = state.shape[1:]
    width = send_list.shape[1]
    entries = loc_ids.shape[1]
    ghosts = 2 * width
    tiles = nodes // LANES
    assert loc_ids.shape[0] == 1
    depth = depth[None]
    place = lax.axis_index("mesh").astype(jnp.int32)[None]
    work = 8 * members * nodes * nodes

    brought = [state, send_list, loc_ids, loc_weight, depth, jnp.swapaxes(coef, 0, 1), wet_faces, conn]
    brought += [obs_nodes, obs_weight, obs_value[None], obs_error[None]]
    near, far, *brought = call(
        send_flow_kernel,
        [shape(2 * members + ROWS, width)] * 2 + [shape(*a.shape, dtype=a.dtype) for a in brought],
        [place, loc_len, *brought],
        scalars=2,
        scratch=[pltpu.SemaphoreType.DMA((len(brought) + 2,))],
        raw=True,
    )
    state, send_list, loc_ids, loc_weight, depth, coef, wet_faces, conn = brought[:8]
    obs_nodes, obs_weight, obs_value, obs_error = brought[8:]
    corners = obs_nodes.shape[0]
    from_far = to_other(far)
    from_near = to_partner(near)
    big = [shape(tiles, nodes, LANES, dtype=BF16)] * 4
    small = [shape(tiles, ghosts, LANES, dtype=BF16)] * 4
    made = call(
        prepare_kernel, big + small + [shape(2, nodes)], [place, coef, wet_faces, conn], scalars=1, flops=2 * work
    )
    operators, ghost_operators, totals = made[:4], made[4:8], made[8]
    field, payload = shape(members, nodes), shape(members, width)
    (partial,) = call(divergence_kernel, [field], [state, *operators, totals], flops=work)
    early = from_near, from_far

    args = [place, state, partial, depth, from_near, from_far, *ghost_operators, send_list]
    level, near, far = call(level_kernel, [field, payload, payload], args, scalars=1, flops=work)
    from_far = to_other(far)
    from_near = to_partner(near)
    east, north = call(slope_kernel, [field] * 2, [level, *operators, totals], flops=work)
    entry_tiles = entries // LANES
    own_high, own_low, tables, found = call(
        sampling_kernel,
        [shape(entry_tiles, nodes, LANES, dtype=BF16)] * 2 + [shape(ROWS, entries), shape(ROWS, 3 * entries)],
        [place, loc_len, *early, loc_ids, loc_weight, obs_nodes, obs_weight, obs_value, obs_error],
        scalars=2,
        scratch=[
            pltpu.VMEM((ROWS, entries), jnp.int32),
            pltpu.VMEM((ROWS, entries), F32),
            pltpu.VMEM((ROWS, obs_nodes.shape[1]), F32),
        ],
        flops=work,
    )

    flow, near, far = call(
        flow_kernel,
        [shape(2, members, nodes)] + [shape(2 * members, width)] * 2,
        [place, state, east, north, from_near, from_far, *ghost_operators, send_list],
        scalars=1,
        flops=work,
    )
    from_far = to_other(far)
    from_near = to_partner(near)
    high, low = call(
        functools.partial(others_kernel, corners),
        [shape(2 * entry_tiles, nodes, LANES, dtype=BF16)] * 2,
        [found],
        flops=work,
    )
    (partial,) = call(divergence_kernel, [field], [flow, *operators, totals], flops=work)

    payload = shape(members + ROWS, width + LANES)
    args = [place, level, partial, depth, from_near, from_far, *ghost_operators, send_list, high, low, tables]
    level, far = call(last_level_kernel, [field, payload], args, scalars=1, flops=work)
    from_far = to_other(far)
    (near,) = call(near_sums_kernel, [payload], [place, level, send_list, high, low, tables], scalars=1, flops=work)
    from_near = to_partner(near)
    east, north = call(slope_kernel, [field] * 2, [level, *operators, totals], flops=work)
    (sums,) = call(own_sums_kernel, [shape(members + ROWS, members)], [level, own_high, own_low, tables], flops=work)
    (out,) = call(
        analysis_kernel,
        [shape(3, members, nodes)],
        [flow, level, east, north, sums, from_near, from_far, *ghost_operators],
        scratch=[
            pltpu.VMEM((3, members, nodes), F32),
            pltpu.VMEM((3, 2 * members, nodes), BF16),
            pltpu.VMEM((ROWS, nodes), F32),
            pltpu.SemaphoreType.DMA((3,)),
        ],
        flops=work,
        final=True,
    )
    return out


def solution(mesh):
    spread = ("groups", "mesh")
    in_specs = (
        P(None, None, spread),
        P(spread),
        P(None, None, spread),
        P(None, spread),
        P(None, spread),
        P(None, spread),
        P(None, spread),
        P(None, spread),
        P(spread),
        P(spread),
        P(spread, None),
        P(spread),
        P(spread, None),
    )
    out_specs = P(None, None, spread)
    return jax.shard_map(local, mesh=mesh, in_specs=in_specs, out_specs=out_specs, check_vma=False)
```

```python
import functools
import math

import jax
import jax.numpy as jnp
from jax import lax
from jax.experimental import pallas as pl
from jax.experimental.pallas import tpu as pltpu
from jax.sharding import PartitionSpec as P

DT = 0.1
LANES = 128
ROWS = 8
F32 = jnp.float32
BF16 = jnp.bfloat16


def halves(value):
    high = value.astype(BF16)
    return high, (value - high.astype(F32)).astype(BF16)


def stacked(value):
    high, low = halves(value)
    return jnp.concatenate([high, low], axis=0)


def product(stack, high, low, first=0, count=None):
    rows = stack.shape[0] // 2
    count = high.shape[0] if count is None else count
    pieces = []
    for tile in range(first, first + count, 2):
        total = 0.0
        for part in (high, low):
            block = jnp.concatenate([part[tile], part[tile + 1]], axis=1)
            total = total + jnp.dot(stack, block, preferred_element_type=F32)
        pieces.append(total[:rows] + total[rows:])
    return jnp.concatenate(pieces, axis=1)


def pick_lanes(sources, indices, targets):
    rows, extent = sources.shape
    plans = []
    for index, target in zip(indices, targets):
        for start in range(0, index.shape[1], LANES):
            wide = jnp.broadcast_to(index[:, start : start + LANES], (ROWS, LANES))
            plans.append((wide & (LANES - 1), wide >> 7, target, start))

    def group(step, carry):
        first = pl.multiple_of(step * ROWS, ROWS)
        for lane, tile, (ref, row0, col0), start in plans:
            total = jnp.zeros((ROWS, LANES), F32)
            for place in range(extent // LANES):
                block = sources[pl.ds(first, ROWS), place * LANES : (place + 1) * LANES]
                found = jnp.take_along_axis(block, lane, axis=1, mode="promise_in_bounds")
                total = jnp.where(tile == place, found, total)
            ref[pl.ds(row0 + first, ROWS), col0 + start : col0 + start + LANES] = total
        return carry

    lax.fori_loop(0, rows // ROWS, group, 0, unroll=True)


def merged(targets, weights):
    targets = list(targets)
    weights = [list(group) for group in weights]
    count = len(targets)
    for first in range(count):
        for second in range(first + 1, count):
            same = targets[first] == targets[second]
            for group in weights:
                group[first] = group[first] + jnp.where(same, group[second], 0.0)
                group[second] = jnp.where(same, 0.0, group[second])
    return weights


def build_operator(targets, weights, outputs, begin, extent, tile):
    count = len(targets)
    tall = 2 * ROWS
    wanted = [jnp.broadcast_to(t - begin, (tall, LANES)).astype(jnp.int16) for t in targets]
    parts = []
    for group in weights:
        for w in group:
            high = w.astype(BF16).astype(F32)
            parts.append(
                (
                    jnp.broadcast_to(high, (tall, LANES)).astype(BF16),
                    jnp.broadcast_to(w - high, (tall, LANES)).astype(BF16),
                )
            )

    def block(step, rows):
        first = pl.multiple_of(step * tall, tall)
        values = [jnp.zeros((tall, LANES), BF16) for _ in range(2 * len(weights))]
        for slot in range(count - 1, -1, -1):
            hit = wanted[slot] == rows
            for g in range(len(weights)):
                high, low = parts[g * count + slot]
                values[2 * g] = jnp.where(hit, high, values[2 * g])
                values[2 * g + 1] = jnp.where(hit, low, values[2 * g + 1])
        for value, ref in zip(values, outputs):
            ref[tile, pl.ds(first, tall), :] = value
        return rows + jnp.int16(tall)

    start = lax.broadcasted_iota(jnp.int32, (tall, LANES), 0).astype(jnp.int16)
    lax.fori_loop(0, extent // tall, block, start, unroll=8 if count > 3 else 32)


def chosen_lists(place, lists):
    odd = place[0] & 1
    return lists[pl.ds(1 - odd, 1), :], lists[pl.ds(odd, 1), :]


def live_weight(weight, length):
    entry = lax.broadcasted_iota(jnp.int32, weight.shape, 1)
    return jnp.where(entry < length, weight, 0.0)


def send_flow_kernel(place, length, *refs):
    count = (len(refs) - 3) // 2
    held, (near, far), kept, arrived = refs[:count], refs[count : count + 2], refs[count + 2 : -1], refs[-1]
    state_at, state, lists, ids, weight = held[0], kept[0], kept[1], kept[2], kept[3]
    members, width = state.shape[1], lists.shape[1]
    pairs = [(held[1], lists), (state_at.at[1], state.at[1]), (state_at.at[2], state.at[2])]
    pairs += list(zip(held[2:], kept[2:])) + [(state_at.at[0], state.at[0])]
    copies = [pltpu.make_async_copy(a, b, arrived.at[n]) for n, (a, b) in enumerate(pairs)]
    for copy in copies:
        copy.start()
    copies[0].wait()
    chosen = chosen_lists(place, lists)
    for part in range(2):
        copies[1 + part].wait()
        pick_lanes(state.at[1 + part], chosen, [(near, part * members, 0), (far, part * members, 0)])
    for copy in copies[3:]:
        copy.wait()
    block = jnp.zeros((near.shape[0] - 2 * members, width), F32)
    row = lax.broadcasted_iota(jnp.int32, block.shape, 0)
    pieces = ids.shape[1] // width
    for at, values in enumerate((ids[...].astype(F32), live_weight(weight[...], length[0]))):
        for piece in range(pieces):
            line = values[:, piece * width : (piece + 1) * width]
            block = jnp.where(row == at * pieces + piece, jnp.broadcast_to(line, block.shape), block)
    near[2 * members :, :] = block
    far[2 * members :, :] = block


def prepare_kernel(place, coef, wet, conn, eh, el, nh, nl, geh, gel, gnh, gnl, totals):
    slots, nodes = conn.shape
    ghosts = geh.shape[1]
    turned = (1 - (place[0] & 1)) * (ghosts // 2)
    for column in range(0, nodes, LANES):
        cut = slice(column, column + LANES)
        targets = []
        for s in range(slots):
            raw = conn[s : s + 1, cut]
            ghost = raw - nodes + turned
            ghost = jnp.where(ghost >= ghosts, ghost - ghosts, ghost)
            targets.append(jnp.where(raw < nodes, raw, nodes + ghost))
        faces = [wet[s : s + 1, cut].astype(F32) for s in range(slots)]
        weights = [[faces[s] * coef[s, d : d + 1, cut] for s in range(slots)] for d in range(2)]
        for d in range(2):
            totals[d : d + 1, cut] = sum(weights[d][1:], weights[d][0])
        weights = merged(targets, weights)
        build_operator(targets, weights, (eh, el, nh, nl), 0, nodes, column // LANES)
        build_operator(targets, weights, (geh, gel, gnh, gnl), nodes, ghosts, column // LANES)


def ghost_flow(near, far, part, members):
    rows = slice(part * members, (part + 1) * members)
    return jnp.concatenate([near[rows, :], far[rows, :]], axis=1)


def stepped_level(held, partial, depth, near, far, geh, gel, gnh, gnl):
    level = held.at[0] if len(held.shape) == 3 else held
    members = level.shape[0]
    divergence = (
        partial[...]
        + product(stacked(ghost_flow(near, far, 0, members)), geh, gel)
        + product(stacked(ghost_flow(near, far, 1, members)), gnh, gnl)
    )
    return level[...] - DT * depth[...] * divergence


def level_kernel(place, held, partial, depth, near, far, geh, gel, gnh, gnl, lists, new_level, to_far):
    new_level[...] = stepped_level(held, partial, depth, near, far, geh, gel, gnh, gnl)
    pick_lanes(new_level, chosen_lists(place, lists)[1:], [(to_far, 0, 0)])


def near_picks_kernel(place, field, lists, to_near):
    chosen = chosen_lists(place, lists)[:1]
    if len(field.shape) == 2:
        pick_lanes(field, chosen, [(to_near, 0, 0)])
    else:
        for part in range(field.shape[0]):
            pick_lanes(field.at[part], chosen, [(to_near, part * field.shape[1], 0)])


def thirds(value):
    high, rest = halves(value)
    middle = rest
    low = (value - high.astype(F32) - middle.astype(F32)).astype(BF16)
    return high, middle, low


def row_products(left, right):
    rows = left.shape[0]
    ours, theirs = thirds(left), thirds(right)
    total = 0.0
    for skip, part in enumerate(theirs):
        block = jnp.concatenate(ours[: 3 - skip], axis=0)
        found = lax.dot_general(block, part, (((1,), (1,)), ((), ())), preferred_element_type=F32)
        sums = [found[at * rows : (at + 1) * rows] for at in range(3 - skip)]
        while len(sums) > 1:
            sums[-2:] = [sums[-2] + sums[-1]]
        total = sums[0] + total
    return total


def list_sums(seen, value, weight):
    obs_mean = jnp.mean(seen, axis=0, keepdims=True)
    anomalies = seen - obs_mean
    pull = jnp.broadcast_to(weight * (value - obs_mean), (ROWS, seen.shape[1]))
    left = jnp.concatenate([anomalies * weight, pull], axis=0)
    return row_products(left, anomalies)


def neighbour_payload(which, place, level, lists, high, low, tables, ref):
    members, width = level.shape[0], lists.shape[1]
    tiles = high.shape[0] // 2
    pick_lanes(level, [chosen_lists(place, lists)[which]], [(ref, 0, 0)])
    seen = product(stacked(level[...]), high, low, which * tiles, tiles)
    sums = list_sums(seen, tables[2 * which : 2 * which + 1, :], tables[2 * which + 1 : 2 * which + 2, :])
    ref[members:, :width] = jnp.zeros((ROWS, width), F32)
    ref[:, width:] = jnp.concatenate([sums, jnp.zeros((members + ROWS, LANES - members), F32)], axis=1)


def last_level_kernel(
    place, held, partial, depth, near, far, geh, gel, gnh, gnl, lists, high, low, tables, new_level, to_far
):
    new_level[...] = stepped_level(held, partial, depth, near, far, geh, gel, gnh, gnl)
    neighbour_payload(1, place, new_level, lists, high, low, tables, to_far)


def near_sums_kernel(place, level, lists, high, low, tables, to_near):
    neighbour_payload(0, place, level, lists, high, low, tables, to_near)


def slope_kernel(level, eh, el, nh, nl, totals, east, north):
    stack = stacked(level[...])
    east[...] = product(stack, eh, el) - level[...] * totals[0:1, :]
    north[...] = product(stack, nh, nl) - level[...] * totals[1:2, :]


def sampling_kernel(
    place, length, near, far, ids, weight, obs_nodes, obs_weight, obs_value, obs_error, high, low, tables, found,
    numbers, strengths, scratch,
):
    entries, width = ids.shape[1], near.shape[1]
    corners, obs_count = obs_nodes.shape
    base = place[0] * obs_count
    scratch[0:corners, :] = obs_nodes[...].astype(F32)
    scratch[corners : 2 * corners, :] = obs_weight[...]
    scratch[2 * corners : 2 * corners + 1, :] = obs_value[...]
    scratch[2 * corners + 1 : 2 * corners + 2, :] = 1.0 / (obs_error[...] * obs_error[...])
    first = near.shape[0] - ROWS
    pieces = entries // width
    for piece in range(pieces):
        cut = slice(piece * width, (piece + 1) * width)
        for owner, ref in enumerate((near, far)):
            at = first + piece
            numbers[owner : owner + 1, cut] = ref[at : at + 1, :].astype(jnp.int32)
            strengths[owner : owner + 1, cut] = ref[at + pieces : at + pieces + 1, :]
    numbers[2:3, :] = ids[...]
    strengths[2:3, :] = live_weight(weight[...], length[0])
    tiles = entries // LANES
    places = [(owner, tile) for owner in range(3) for tile in range(tiles)]
    kept = {}
    for owner, tile in places:
        index = numbers[owner : owner + 1, tile * LANES : (tile + 1) * LANES] - base
        own = (index >= 0) & (index < obs_count)
        kept[owner, tile] = own, jnp.where(own, index, 0)
    pick_lanes(
        scratch,
        [kept[spot][1] for spot in places],
        [(found, 0, (owner * tiles + tile) * LANES) for owner, tile in places],
    )
    for owner, tile in places:
        at = slice((owner * tiles + tile) * LANES, (owner * tiles + tile + 1) * LANES)
        own = kept[owner, tile][0]
        cut = slice(tile * LANES, (tile + 1) * LANES)
        found[corners : 2 * corners, at] = jnp.where(own, found[corners : 2 * corners, at], 0.0)
        force = found[2 * corners + 1 : 2 * corners + 2, at] * strengths[owner : owner + 1, cut]
        tables[2 * owner : 2 * owner + 1, cut] = found[2 * corners : 2 * corners + 1, at]
        tables[2 * owner + 1 : 2 * owner + 2, cut] = jnp.where(own, force, 0.0)
    corner_operator(found, 2 * tiles, corners, high, low)


def corner_operator(found, first, corners, high, low):
    for tile in range(high.shape[0]):
        here = found[:, (first + tile) * LANES : (first + tile + 1) * LANES]
        targets = [here[c : c + 1, :].astype(jnp.int32) for c in range(corners)]
        shares = [here[corners + c : corners + c + 1, :] for c in range(corners)]
        build_operator(targets, merged(targets, [shares]), (high, low), 0, high.shape[1], tile)


def others_kernel(corners, found, high, low):
    corner_operator(found, 0, corners, high, low)


def flow_kernel(place, flow, east, north, near, far, geh, gel, gnh, gnl, lists, new_flow, to_far):
    members = east.shape[0]
    stack = stacked(jnp.concatenate([near[...], far[...]], axis=1))
    chosen = chosen_lists(place, lists)[1:]
    first = flow.shape[0] - 2
    new_flow[0] = flow[first] - DT * (east[...] + product(stack, geh, gel))
    new_flow[1] = flow[first + 1] - DT * (north[...] + product(stack, gnh, gnl))
    for part in range(2):
        pick_lanes(new_flow.at[part], chosen, [(to_far, part * members, 0)])


def divergence_kernel(flow, eh, el, nh, nl, totals, partial):
    first = flow.shape[0] - 2
    east, north = flow[first], flow[first + 1]
    partial[...] = (
        product(stacked(east), eh, el)
        + product(stacked(north), nh, nl)
        - east * totals[0:1, :]
        - north * totals[1:2, :]
    )


def own_sums_kernel(level, high, low, tables, sums):
    sums[...] = list_sums(product(stacked(level[...]), high, low), tables[4:5, :], tables[5:6, :])


def pair_inverse(a, b, c):
    r = 1.0 / (a * c - b * b)
    return c * r, -(b * r), a * r


def pair_rows(a, b, c, first, second):
    m = b / a
    return first * lax.rsqrt(a), (second - m * first) * lax.rsqrt(c - m * b)


def inverse_factor(gram, beside):
    size = gram.shape[0]
    wide = (ROWS, 2 * size)
    row = lax.broadcasted_iota(jnp.int32, (size, size), 0)
    col = lax.broadcasted_iota(jnp.int32, (size, size), 1)
    table = jnp.concatenate([gram, (row == col).astype(F32)], axis=1)
    blocks = [table[b : b + ROWS, :] for b in range(0, size, ROWS)]
    inner = lax.broadcasted_iota(jnp.int32, wide, 0)

    def spread(value):
        return jnp.broadcast_to(value, wide)

    def columns_of(block, pivot):
        return [spread(block[:, pivot + i : pivot + i + 1]) for i in range(ROWS)]

    done = []
    for home in range(len(blocks)):
        pivot = home * ROWS
        lines = [spread(blocks[home][i : i + 1, :]) for i in range(ROWS)]
        columns = columns_of(blocks[home], pivot)
        entry = {(i, j): spread(columns[j][i : i + 1, :]) for i in range(ROWS) for j in range(i + 1)}
        inverses, factors = {}, {}
        result = jnp.zeros(wide, F32)
        for k in range(0, ROWS, 2):
            head = entry[k, k], entry[k + 1, k], entry[k + 1, k + 1]
            p = inverses[k] = pair_inverse(*head)
            for i, value in enumerate(pair_rows(*head, lines[k], lines[k + 1])):
                result = jnp.where(inner == k + i, value, result)
            for r in range(k + 2, ROWS):
                u, v = entry[r, k], entry[r, k + 1]
                t = factors[r, k] = u * p[0] + v * p[1], u * p[1] + v * p[2]
                for c in range(k + 2, r + 1):
                    entry[r, c] = entry[r, c] - (t[0] * entry[c, k] + t[1] * entry[c, k + 1])
                lines[r] = lines[r] - (t[0] * lines[k] + t[1] * lines[k + 1])
        done.append(result)
        z = [None] * ROWS
        for k in range(ROWS - 2, -1, -2):
            p = inverses[k]
            z[k] = p[0] * lines[k] + p[1] * lines[k + 1]
            z[k + 1] = p[1] * lines[k] + p[2] * lines[k + 1]
            for r in range(k + 2, ROWS):
                z[k] = z[k] - factors[r, k][0] * z[r]
                z[k + 1] = z[k + 1] - factors[r, k][1] * z[r]
        for place in range(home + 1, len(blocks)):
            terms = [f * z[i] for i, f in enumerate(columns_of(blocks[place], pivot))]
            while len(terms) > 1:
                terms = [terms[i] + terms[i + 1] for i in range(0, len(terms), 2)]
            blocks[place] = blocks[place] - terms[0]
        beside()
    return jnp.concatenate(done, axis=0)[:, size:]


def analysis_kernel(
    flow, level, east, north, sums, near, far, geh, gel, gnh, gnl, out, result, moved, averages, sent
):
    members, nodes = level.shape
    width = near.shape[1] - LANES
    total = sums[...] + near[:, width : width + members] + far[:, width : width + members]
    row = lax.broadcasted_iota(jnp.int32, (members, members), 0)
    col = lax.broadcasted_iota(jnp.int32, (members, members), 1)
    gram = total[:members] + jnp.where(row == col, members - 1.0, 0.0)
    rhs = total[members : members + 1]
    stack = stacked(jnp.concatenate([near[:members, :width], far[:members, :width]], axis=1))
    operators = ((geh, gel), (gnh, gnl))

    def piece(part, tile):
        cut = slice(tile * LANES, (tile + 2) * LANES)
        if part == 0:
            field = level[:, cut]
        else:
            slope = (east, north)[part - 1][:, cut] + product(stack, *operators[part - 1], tile, 2)
            field = flow[part - 1, :, cut] - DT * slope
        average = jnp.mean(field, axis=0, keepdims=True)
        moved[part, :, cut] = stacked(field - average)
        averages[part : part + 1, cut] = average

    pieces = [(part, tile) for part in (1, 2, 0) for tile in range(0, nodes // LANES, 2)]

    def beside():
        for _ in range(2):
            if pieces:
                piece(*pieces.pop(0))

    inverse = inverse_factor(gram, beside)
    while pieces:
        beside()
    halfway = jnp.sum(inverse * rhs, axis=1, keepdims=True)
    mean_w = jnp.sum(inverse * halfway, axis=0, keepdims=True)
    blend = math.sqrt(members - 1.0) * inverse + mean_w
    blend = stacked(jnp.concatenate([blend, blend], axis=1))
    copies = []
    for part in range(3):
        change = jnp.dot(blend, moved[part], preferred_element_type=F32)
        result[part] = averages[part : part + 1, :] + (change[:members] + change[members:])
        copies.append(pltpu.make_async_copy(result.at[part], out.at[part], sent.at[part]))
        copies[-1].start()
    for copy in copies:
        copy.wait()


def call(kernel, outs, args, scalars=0, scratch=(), flops=0, final=False, limit=16, raw=False):
    vmem = pl.BlockSpec(memory_space=pltpu.VMEM)
    in_specs = [pl.BlockSpec(memory_space=pltpu.SMEM)] * scalars + [pl.BlockSpec(memory_space=pltpu.HBM) if raw else vmem] * (len(args) - scalars)
    held = sum(math.prod(a.shape) * a.dtype.itemsize for a in list(args) + list(outs))
    if not final:
        outs = [pltpu.VMEM(o.shape, o.dtype) for o in outs]
    space = pltpu.HBM if raw else pltpu.VMEM
    args = list(args[:scalars]) + [pltpu.with_memory_space_constraint(a, space) for a in args[scalars:]]
    return pl.pallas_call(
        kernel,
        out_shape=outs,
        in_specs=in_specs,
        out_specs=[pl.BlockSpec(memory_space=pltpu.HBM) if final else vmem] * len(outs),
        scratch_shapes=scratch,
        compiler_params=pltpu.CompilerParams(vmem_limit_bytes=limit << 20),
        cost_estimate=pl.CostEstimate(flops=flops, bytes_accessed=held, transcendentals=0),
    )(*args)


def shape(*dims, dtype=F32):
    return jax.ShapeDtypeStruct(dims, dtype)


def to_partner(value):
    pairs = [(i, i ^ 1) for i in range(lax.axis_size("mesh"))]
    return lax.ppermute(value, "mesh", pairs)


def to_other(value):
    count = lax.axis_size("mesh")
    others = [(i, ((i + 1) ^ 1) - 1) for i in range(1, count - 1)]
    return lax.ppermute(value, "mesh", others)


def local(
    state,
    depth,
    coef,
    wet_faces,
    conn,
    send_list,
    obs_nodes,
    obs_weight,
    obs_value,
    obs_error,
    loc_ids,
    loc_len,
    loc_weight,
):
    members, nodes = state.shape[1:]
    width = send_list.shape[1]
    entries = loc_ids.shape[1]
    ghosts = 2 * width
    tiles = nodes // LANES
    assert loc_ids.shape[0] == 1
    depth = depth[None]
    place = lax.axis_index("mesh").astype(jnp.int32)[None]
    work = 8 * members * nodes * nodes

    brought = [state, send_list, loc_ids, loc_weight, depth, jnp.swapaxes(coef, 0, 1), wet_faces, conn]
    brought += [obs_nodes, obs_weight, obs_value[None], obs_error[None]]
    near, far, *brought = call(
        send_flow_kernel,
        [shape(2 * members + ROWS, width)] * 2 + [shape(*a.shape, dtype=a.dtype) for a in brought],
        [place, loc_len, *brought],
        scalars=2,
        scratch=[pltpu.SemaphoreType.DMA((len(brought) + 2,))],
        raw=True,
    )
    state, send_list, loc_ids, loc_weight, depth, coef, wet_faces, conn = brought[:8]
    obs_nodes, obs_weight, obs_value, obs_error = brought[8:]
    corners = obs_nodes.shape[0]
    from_far = to_other(far)
    from_near = to_partner(near)
    big = [shape(tiles, nodes, LANES, dtype=BF16)] * 4
    small = [shape(tiles, ghosts, LANES, dtype=BF16)] * 4
    made = call(
        prepare_kernel, big + small + [shape(2, nodes)], [place, coef, wet_faces, conn], scalars=1, flops=2 * work
    )
    operators, ghost_operators, totals = made[:4], made[4:8], made[8]
    field, payload = shape(members, nodes), shape(members, width)
    (partial,) = call(divergence_kernel, [field], [state, *operators, totals], flops=work)
    early = from_near, from_far

    args = [place, state, partial, depth, from_near, from_far, *ghost_operators, send_list]
    level, far = call(level_kernel, [field, payload], args, scalars=1, flops=work)
    from_far = to_other(far)
    (near,) = call(near_picks_kernel, [payload], [place, level, send_list], scalars=1)
    from_near = to_partner(near)
    east, north = call(slope_kernel, [field] * 2, [level, *operators, totals], flops=work)
    entry_tiles = entries // LANES
    own_high, own_low, tables, found = call(
        sampling_kernel,
        [shape(entry_tiles, nodes, LANES, dtype=BF16)] * 2 + [shape(ROWS, entries), shape(ROWS, 3 * entries)],
        [place, loc_len, *early, loc_ids, loc_weight, obs_nodes, obs_weight, obs_value, obs_error],
        scalars=2,
        scratch=[
            pltpu.VMEM((ROWS, entries), jnp.int32),
            pltpu.VMEM((ROWS, entries), F32),
            pltpu.VMEM((ROWS, obs_nodes.shape[1]), F32),
        ],
        flops=work,
    )

    flow, far = call(
        flow_kernel,
        [shape(2, members, nodes), shape(2 * members, width)],
        [place, state, east, north, from_near, from_far, *ghost_operators, send_list],
        scalars=1,
        flops=work,
    )
    from_far = to_other(far)
    (near,) = call(near_picks_kernel, [shape(2 * members, width)], [place, flow, send_list], scalars=1)
    from_near = to_partner(near)
    high, low = call(
        functools.partial(others_kernel, corners),
        [shape(2 * entry_tiles, nodes, LANES, dtype=BF16)] * 2,
        [found],
        flops=work,
    )
    (partial,) = call(divergence_kernel, [field], [flow, *operators, totals], flops=work)

    payload = shape(members + ROWS, width + LANES)
    args = [place, level, partial, depth, from_near, from_far, *ghost_operators, send_list, high, low, tables]
    level, far = call(last_level_kernel, [field, payload], args, scalars=1, flops=work)
    from_far = to_other(far)
    (near,) = call(near_sums_kernel, [payload], [place, level, send_list, high, low, tables], scalars=1, flops=work)
    from_near = to_partner(near)
    east, north = call(slope_kernel, [field] * 2, [level, *operators, totals], flops=work)
    (sums,) = call(own_sums_kernel, [shape(members + ROWS, members)], [level, own_high, own_low, tables], flops=work)
    (out,) = call(
        analysis_kernel,
        [shape(3, members, nodes)],
        [flow, level, east, north, sums, from_near, from_far, *ghost_operators],
        scratch=[
            pltpu.VMEM((3, members, nodes), F32),
            pltpu.VMEM((3, 2 * members, nodes), BF16),
            pltpu.VMEM((ROWS, nodes), F32),
            pltpu.SemaphoreType.DMA((3,)),
        ],
        flops=work,
        final=True,
    )
    return out


def solution(mesh):
    spread = ("groups", "mesh")
    in_specs = (
        P(None, None, spread),
        P(spread),
        P(None, None, spread),
        P(None, spread),
        P(None, spread),
        P(None, spread),
        P(None, spread),
        P(None, spread),
        P(spread),
        P(spread),
        P(spread, None),
        P(spread),
        P(spread, None),
    )
    out_specs = P(None, None, spread)
    return jax.shard_map(local, mesh=mesh, in_specs=in_specs, out_specs=out_specs, check_vma=False)
```

```python
import functools
import math

import jax
import jax.numpy as jnp
from jax import lax
from jax.experimental import pallas as pl
from jax.experimental.pallas import tpu as pltpu
from jax.sharding import PartitionSpec as P

DT = 0.1
LANES = 128
ROWS = 8
F32 = jnp.float32
BF16 = jnp.bfloat16


def halves(value):
    high = value.astype(BF16)
    return high, (value - high.astype(F32)).astype(BF16)


def stacked(value):
    high, low = halves(value)
    return jnp.concatenate([high, low], axis=0)


def product(stack, high, low, first=0, count=None):
    rows = stack.shape[0] // 2
    count = high.shape[0] if count is None else count
    pieces = []
    for tile in range(first, first + count, 2):
        total = 0.0
        for part in (high, low):
            block = jnp.concatenate([part[tile], part[tile + 1]], axis=1)
            total = total + jnp.dot(stack, block, preferred_element_type=F32)
        pieces.append(total[:rows] + total[rows:])
    return jnp.concatenate(pieces, axis=1)


def pick_lanes(sources, indices, targets):
    rows, extent = sources.shape
    plans = []
    for index, target in zip(indices, targets):
        for start in range(0, index.shape[1], LANES):
            wide = jnp.broadcast_to(index[:, start : start + LANES], (ROWS, LANES))
            plans.append((wide & (LANES - 1), wide >> 7, target, start))

    def group(step, carry):
        first = pl.multiple_of(step * ROWS, ROWS)
        for lane, tile, (ref, row0, col0), start in plans:
            total = jnp.zeros((ROWS, LANES), F32)
            for place in range(extent // LANES):
                block = sources[pl.ds(first, ROWS), place * LANES : (place + 1) * LANES]
                found = jnp.take_along_axis(block, lane, axis=1, mode="promise_in_bounds")
                total = jnp.where(tile == place, found, total)
            ref[pl.ds(row0 + first, ROWS), col0 + start : col0 + start + LANES] = total
        return carry

    lax.fori_loop(0, rows // ROWS, group, 0, unroll=True)


def merged(targets, weights):
    targets = list(targets)
    weights = [list(group) for group in weights]
    count = len(targets)
    for first in range(count):
        for second in range(first + 1, count):
            same = targets[first] == targets[second]
            for group in weights:
                group[first] = group[first] + jnp.where(same, group[second], 0.0)
                group[second] = jnp.where(same, 0.0, group[second])
    return weights


def build_operator(targets, weights, outputs, begin, extent, tile, unroll):
    count = len(targets)
    tall = 2 * ROWS
    wanted = [jnp.broadcast_to(t - begin, (tall, LANES)).astype(jnp.int16) for t in targets]
    parts = []
    for group in weights:
        for w in group:
            high = w.astype(BF16).astype(F32)
            parts.append(
                (
                    jnp.broadcast_to(high, (tall, LANES)).astype(BF16),
                    jnp.broadcast_to(w - high, (tall, LANES)).astype(BF16),
                )
            )

    def block(step, rows):
        first = pl.multiple_of(step * tall, tall)
        values = [jnp.zeros((tall, LANES), BF16) for _ in range(2 * len(weights))]
        for slot in range(count - 1, -1, -1):
            hit = wanted[slot] == rows
            for g in range(len(weights)):
                high, low = parts[g * count + slot]
                values[2 * g] = jnp.where(hit, high, values[2 * g])
                values[2 * g + 1] = jnp.where(hit, low, values[2 * g + 1])
        for value, ref in zip(values, outputs):
            ref[tile, pl.ds(first, tall), :] = value
        return rows + jnp.int16(tall)

    start = lax.broadcasted_iota(jnp.int32, (tall, LANES), 0).astype(jnp.int16)
    lax.fori_loop(0, extent // tall, block, start, unroll=unroll)


def chosen_lists(place, lists):
    odd = place[0] & 1
    return lists[pl.ds(1 - odd, 1), :], lists[pl.ds(odd, 1), :]


def live_weight(weight, length):
    entry = lax.broadcasted_iota(jnp.int32, weight.shape, 1)
    return jnp.where(entry < length, weight, 0.0)


def send_flow_kernel(place, length, *refs):
    count = (len(refs) - 3) // 2
    held, (near, far), kept, arrived = refs[:count], refs[count : count + 2], refs[count + 2 : -1], refs[-1]
    state_at, state, lists, ids, weight = held[0], kept[0], kept[1], kept[2], kept[3]
    members, width = state.shape[1], lists.shape[1]
    pairs = [(held[1], lists), (state_at.at[1], state.at[1]), (state_at.at[2], state.at[2])]
    pairs += list(zip(held[2:], kept[2:])) + [(state_at.at[0], state.at[0])]
    copies = [pltpu.make_async_copy(a, b, arrived.at[n]) for n, (a, b) in enumerate(pairs)]
    for copy in copies:
        copy.start()
    copies[0].wait()
    chosen = chosen_lists(place, lists)
    for part in range(2):
        copies[1 + part].wait()
        pick_lanes(state.at[1 + part], chosen, [(near, part * members, 0), (far, part * members, 0)])
    for copy in copies[3:]:
        copy.wait()
    block = jnp.zeros((near.shape[0] - 2 * members, width), F32)
    row = lax.broadcasted_iota(jnp.int32, block.shape, 0)
    pieces = ids.shape[1] // width
    for at, values in enumerate((ids[...].astype(F32), live_weight(weight[...], length[0]))):
        for piece in range(pieces):
            line = values[:, piece * width : (piece + 1) * width]
            block = jnp.where(row == at * pieces + piece, jnp.broadcast_to(line, block.shape), block)
    near[2 * members :, :] = block
    far[2 * members :, :] = block


def prepare_kernel(
    place, state, coef, wet, conn, eh, el, nh, nl, geh, gel, gnh, gnl, totals, partial, stacks, targets_at, weights_at
):
    slots, nodes = conn.shape
    ghosts = geh.shape[1]
    turned = (1 - (place[0] & 1)) * (ghosts // 2)
    count = nodes // LANES
    for tile in range(count):
        cut = slice(tile * LANES, (tile + 1) * LANES)
        targets = []
        for s in range(slots):
            raw = conn[s : s + 1, cut]
            ghost = raw - nodes + turned
            ghost = jnp.where(ghost >= ghosts, ghost - ghosts, ghost)
            targets.append(jnp.where(raw < nodes, raw, nodes + ghost))
        faces = [wet[s : s + 1, cut].astype(F32) for s in range(slots)]
        weights = [[faces[s] * coef[s, d : d + 1, cut] for s in range(slots)] for d in range(2)]
        for d in range(2):
            totals[d : d + 1, cut] = sum(weights[d][1:], weights[d][0])
        weights = merged(targets, weights)
        for s in range(slots):
            targets_at[s : s + 1, cut] = targets[s]
            for d in range(2):
                weights_at[d, s : s + 1, cut] = weights[d][s]
        build_operator(targets, weights, (eh, el, nh, nl), 0, nodes, tile, 8)
    for d in range(2):
        stacks[d] = stacked(state[1 + d])
    for tile in range(count):
        pair, d = divmod(tile, 2)
        span = slice(2 * pair * LANES, 2 * (pair + 1) * LANES)
        found = product(stacks[d], *((eh, el), (nh, nl))[d], 2 * pair, 2) - state[1 + d, :, span] * totals[d : d + 1, span]
        cut = slice(tile * LANES, (tile + 1) * LANES)
        targets = [targets_at[s : s + 1, cut] for s in range(slots)]
        weights = [[weights_at[g, s : s + 1, cut] for s in range(slots)] for g in range(2)]
        build_operator(targets, weights, (geh, gel, gnh, gnl), nodes, ghosts, tile, True)
        partial[:, span] = found if d == 0 else partial[:, span] + found


def ghost_flow(near, far, part, members):
    rows = slice(part * members, (part + 1) * members)
    return jnp.concatenate([near[rows, :], far[rows, :]], axis=1)


def stepped_level(held, partial, depth, near, far, geh, gel, gnh, gnl):
    level = held.at[0] if len(held.shape) == 3 else held
    members = level.shape[0]
    divergence = (
        partial[...]
        + product(stacked(ghost_flow(near, far, 0, members)), geh, gel)
        + product(stacked(ghost_flow(near, far, 1, members)), gnh, gnl)
    )
    return level[...] - DT * depth[...] * divergence


def level_kernel(place, held, partial, depth, near, far, geh, gel, gnh, gnl, lists, new_level, to_far):
    new_level[...] = stepped_level(held, partial, depth, near, far, geh, gel, gnh, gnl)
    pick_lanes(new_level, chosen_lists(place, lists)[1:], [(to_far, 0, 0)])


def near_picks_kernel(place, field, lists, to_near):
    chosen = chosen_lists(place, lists)[:1]
    if len(field.shape) == 2:
        pick_lanes(field, chosen, [(to_near, 0, 0)])
    else:
        for part in range(field.shape[0]):
            pick_lanes(field.at[part], chosen, [(to_near, part * field.shape[1], 0)])


def thirds(value):
    high, rest = halves(value)
    middle = rest
    low = (value - high.astype(F32) - middle.astype(F32)).astype(BF16)
    return high, middle, low


def row_products(left, right):
    rows = left.shape[0]
    ours, theirs = thirds(left), thirds(right)
    total = 0.0
    for skip, part in enumerate(theirs):
        block = jnp.concatenate(ours[: 3 - skip], axis=0)
        found = lax.dot_general(block, part, (((1,), (1,)), ((), ())), preferred_element_type=F32)
        sums = [found[at * rows : (at + 1) * rows] for at in range(3 - skip)]
        while len(sums) > 1:
            sums[-2:] = [sums[-2] + sums[-1]]
        total = sums[0] + total
    return total


def list_sums(seen, value, weight):
    obs_mean = jnp.mean(seen, axis=0, keepdims=True)
    anomalies = seen - obs_mean
    pull = jnp.broadcast_to(weight * (value - obs_mean), (ROWS, seen.shape[1]))
    left = jnp.concatenate([anomalies * weight, pull], axis=0)
    return row_products(left, anomalies)


def neighbour_payload(which, place, level, lists, high, low, tables, ref):
    members, width = level.shape[0], lists.shape[1]
    tiles = high.shape[0] // 2
    pick_lanes(level, [chosen_lists(place, lists)[which]], [(ref, 0, 0)])
    seen = product(stacked(level[...]), high, low, which * tiles, tiles)
    sums = list_sums(seen, tables[2 * which : 2 * which + 1, :], tables[2 * which + 1 : 2 * which + 2, :])
    ref[members:, :width] = jnp.zeros((ROWS, width), F32)
    ref[:, width:] = jnp.concatenate([sums, jnp.zeros((members + ROWS, LANES - members), F32)], axis=1)


def last_level_kernel(
    place, held, partial, depth, near, far, geh, gel, gnh, gnl, lists, high, low, tables, new_level, to_far
):
    new_level[...] = stepped_level(held, partial, depth, near, far, geh, gel, gnh, gnl)
    neighbour_payload(1, place, new_level, lists, high, low, tables, to_far)


def near_sums_kernel(place, level, lists, high, low, tables, to_near):
    neighbour_payload(0, place, level, lists, high, low, tables, to_near)


def slope_kernel(level, eh, el, nh, nl, totals, east, north):
    stack = stacked(level[...])
    east[...] = product(stack, eh, el) - level[...] * totals[0:1, :]
    north[...] = product(stack, nh, nl) - level[...] * totals[1:2, :]


def sampling_kernel(
    place, length, near, far, ids, weight, obs_nodes, obs_weight, obs_value, obs_error, high, low, tables, found,
    numbers, strengths, scratch,
):
    entries, width = ids.shape[1], near.shape[1]
    corners, obs_count = obs_nodes.shape
    base = place[0] * obs_count
    scratch[0:corners, :] = obs_nodes[...].astype(F32)
    scratch[corners : 2 * corners, :] = obs_weight[...]
    scratch[2 * corners : 2 * corners + 1, :] = obs_value[...]
    scratch[2 * corners + 1 : 2 * corners + 2, :] = 1.0 / (obs_error[...] * obs_error[...])
    first = near.shape[0] - ROWS
    pieces = entries // width
    for piece in range(pieces):
        cut = slice(piece * width, (piece + 1) * width)
        for owner, ref in enumerate((near, far)):
            at = first + piece
            numbers[owner : owner + 1, cut] = ref[at : at + 1, :].astype(jnp.int32)
            strengths[owner : owner + 1, cut] = ref[at + pieces : at + pieces + 1, :]
    numbers[2:3, :] = ids[...]
    strengths[2:3, :] = live_weight(weight[...], length[0])
    tiles = entries // LANES
    places = [(owner, tile) for owner in range(3) for tile in range(tiles)]
    kept = {}
    for owner, tile in places:
        index = numbers[owner : owner + 1, tile * LANES : (tile + 1) * LANES] - base
        own = (index >= 0) & (index < obs_count)
        kept[owner, tile] = own, jnp.where(own, index, 0)
    pick_lanes(
        scratch,
        [kept[spot][1] for spot in places],
        [(found, 0, (owner * tiles + tile) * LANES) for owner, tile in places],
    )
    for owner, tile in places:
        at = slice((owner * tiles + tile) * LANES, (owner * tiles + tile + 1) * LANES)
        own = kept[owner, tile][0]
        cut = slice(tile * LANES, (tile + 1) * LANES)
        found[corners : 2 * corners, at] = jnp.where(own, found[corners : 2 * corners, at], 0.0)
        force = found[2 * corners + 1 : 2 * corners + 2, at] * strengths[owner : owner + 1, cut]
        tables[2 * owner : 2 * owner + 1, cut] = found[2 * corners : 2 * corners + 1, at]
        tables[2 * owner + 1 : 2 * owner + 2, cut] = jnp.where(own, force, 0.0)
    corner_operator(found, 2 * tiles, corners, high, low)


def corner_operator(found, first, corners, high, low):
    for tile in range(high.shape[0]):
        here = found[:, (first + tile) * LANES : (first + tile + 1) * LANES]
        targets = [here[c : c + 1, :].astype(jnp.int32) for c in range(corners)]
        shares = [here[corners + c : corners + c + 1, :] for c in range(corners)]
        build_operator(targets, merged(targets, [shares]), (high, low), 0, high.shape[1], tile, 32)


def others_kernel(corners, found, high, low):
    corner_operator(found, 0, corners, high, low)


def flow_kernel(place, flow, east, north, near, far, geh, gel, gnh, gnl, lists, new_flow, to_far):
    members = east.shape[0]
    stack = stacked(jnp.concatenate([near[...], far[...]], axis=1))
    chosen = chosen_lists(place, lists)[1:]
    first = flow.shape[0] - 2
    new_flow[0] = flow[first] - DT * (east[...] + product(stack, geh, gel))
    new_flow[1] = flow[first + 1] - DT * (north[...] + product(stack, gnh, gnl))
    for part in range(2):
        pick_lanes(new_flow.at[part], chosen, [(to_far, part * members, 0)])


def divergence_kernel(flow, eh, el, nh, nl, totals, partial):
    first = flow.shape[0] - 2
    east, north = flow[first], flow[first + 1]
    partial[...] = (
        product(stacked(east), eh, el)
        + product(stacked(north), nh, nl)
        - east * totals[0:1, :]
        - north * totals[1:2, :]
    )


def own_sums_kernel(level, high, low, tables, sums):
    sums[...] = list_sums(product(stacked(level[...]), high, low), tables[4:5, :], tables[5:6, :])


def pair_inverse(a, b, c):
    r = 1.0 / (a * c - b * b)
    return c * r, -(b * r), a * r


def pair_rows(a, b, c, first, second):
    m = b / a
    return first * lax.rsqrt(a), (second - m * first) * lax.rsqrt(c - m * b)


def inverse_factor(gram, beside):
    size = gram.shape[0]
    wide = (ROWS, 2 * size)
    row = lax.broadcasted_iota(jnp.int32, (size, size), 0)
    col = lax.broadcasted_iota(jnp.int32, (size, size), 1)
    table = jnp.concatenate([gram, (row == col).astype(F32)], axis=1)
    blocks = [table[b : b + ROWS, :] for b in range(0, size, ROWS)]
    inner = lax.broadcasted_iota(jnp.int32, wide, 0)

    def spread(value):
        return jnp.broadcast_to(value, wide)

    def columns_of(block, pivot):
        return [spread(block[:, pivot + i : pivot + i + 1]) for i in range(ROWS)]

    done = []
    for home in range(len(blocks)):
        pivot = home * ROWS
        lines = [spread(blocks[home][i : i + 1, :]) for i in range(ROWS)]
        columns = columns_of(blocks[home], pivot)
        entry = {(i, j): spread(columns[j][i : i + 1, :]) for i in range(ROWS) for j in range(i + 1)}
        inverses, factors = {}, {}
        result = jnp.zeros(wide, F32)
        for k in range(0, ROWS, 2):
            head = entry[k, k], entry[k + 1, k], entry[k + 1, k + 1]
            p = inverses[k] = pair_inverse(*head)
            for i, value in enumerate(pair_rows(*head, lines[k], lines[k + 1])):
                result = jnp.where(inner == k + i, value, result)
            for r in range(k + 2, ROWS):
                u, v = entry[r, k], entry[r, k + 1]
                t = factors[r, k] = u * p[0] + v * p[1], u * p[1] + v * p[2]
                for c in range(k + 2, r + 1):
                    entry[r, c] = entry[r, c] - (t[0] * entry[c, k] + t[1] * entry[c, k + 1])
                lines[r] = lines[r] - (t[0] * lines[k] + t[1] * lines[k + 1])
        done.append(result)
        z = [None] * ROWS
        for k in range(ROWS - 2, -1, -2):
            p = inverses[k]
            z[k] = p[0] * lines[k] + p[1] * lines[k + 1]
            z[k + 1] = p[1] * lines[k] + p[2] * lines[k + 1]
            for r in range(k + 2, ROWS):
                z[k] = z[k] - factors[r, k][0] * z[r]
                z[k + 1] = z[k + 1] - factors[r, k][1] * z[r]
        for place in range(home + 1, len(blocks)):
            terms = [f * z[i] for i, f in enumerate(columns_of(blocks[place], pivot))]
            while len(terms) > 1:
                terms = [terms[i] + terms[i + 1] for i in range(0, len(terms), 2)]
            blocks[place] = blocks[place] - terms[0]
        beside()
    return jnp.concatenate(done, axis=0)[:, size:]


def analysis_kernel(
    flow, level, east, north, sums, near, far, geh, gel, gnh, gnl, out, result, moved, averages, sent
):
    members, nodes = level.shape
    width = near.shape[1] - LANES
    total = sums[...] + near[:, width : width + members] + far[:, width : width + members]
    row = lax.broadcasted_iota(jnp.int32, (members, members), 0)
    col = lax.broadcasted_iota(jnp.int32, (members, members), 1)
    gram = total[:members] + jnp.where(row == col, members - 1.0, 0.0)
    rhs = total[members : members + 1]
    stack = stacked(jnp.concatenate([near[:members, :width], far[:members, :width]], axis=1))
    operators = ((geh, gel), (gnh, gnl))

    def piece(part, tile):
        cut = slice(tile * LANES, (tile + 2) * LANES)
        if part == 0:
            field = level[:, cut]
        else:
            slope = (east, north)[part - 1][:, cut] + product(stack, *operators[part - 1], tile, 2)
            field = flow[part - 1, :, cut] - DT * slope
        average = jnp.mean(field, axis=0, keepdims=True)
        moved[part, :, cut] = stacked(field - average)
        averages[part : part + 1, cut] = average

    pieces = [(part, tile) for part in (1, 2, 0) for tile in range(0, nodes // LANES, 2)]

    def beside():
        for _ in range(2):
            if pieces:
                piece(*pieces.pop(0))

    inverse = inverse_factor(gram, beside)
    while pieces:
        beside()
    halfway = jnp.sum(inverse * rhs, axis=1, keepdims=True)
    mean_w = jnp.sum(inverse * halfway, axis=0, keepdims=True)
    blend = math.sqrt(members - 1.0) * inverse + mean_w
    blend = stacked(jnp.concatenate([blend, blend], axis=1))
    copies = []
    for part in range(3):
        change = jnp.dot(blend, moved[part], preferred_element_type=F32)
        result[part] = averages[part : part + 1, :] + (change[:members] + change[members:])
        copies.append(pltpu.make_async_copy(result.at[part], out.at[part], sent.at[part]))
        copies[-1].start()
    for copy in copies:
        copy.wait()


def call(kernel, outs, args, scalars=0, scratch=(), flops=0, final=False, limit=16, raw=False):
    vmem = pl.BlockSpec(memory_space=pltpu.VMEM)
    in_specs = [pl.BlockSpec(memory_space=pltpu.SMEM)] * scalars + [pl.BlockSpec(memory_space=pltpu.HBM) if raw else vmem] * (len(args) - scalars)
    held = sum(math.prod(a.shape) * a.dtype.itemsize for a in list(args) + list(outs))
    if not final:
        outs = [pltpu.VMEM(o.shape, o.dtype) for o in outs]
    space = pltpu.HBM if raw else pltpu.VMEM
    args = list(args[:scalars]) + [pltpu.with_memory_space_constraint(a, space) for a in args[scalars:]]
    return pl.pallas_call(
        kernel,
        out_shape=outs,
        in_specs=in_specs,
        out_specs=[pl.BlockSpec(memory_space=pltpu.HBM) if final else vmem] * len(outs),
        scratch_shapes=scratch,
        compiler_params=pltpu.CompilerParams(vmem_limit_bytes=limit << 20),
        cost_estimate=pl.CostEstimate(flops=flops, bytes_accessed=held, transcendentals=0),
    )(*args)


def shape(*dims, dtype=F32):
    return jax.ShapeDtypeStruct(dims, dtype)


def to_partner(value):
    pairs = [(i, i ^ 1) for i in range(lax.axis_size("mesh"))]
    return lax.ppermute(value, "mesh", pairs)


def to_other(value):
    count = lax.axis_size("mesh")
    others = [(i, ((i + 1) ^ 1) - 1) for i in range(1, count - 1)]
    return lax.ppermute(value, "mesh", others)


def local(
    state,
    depth,
    coef,
    wet_faces,
    conn,
    send_list,
    obs_nodes,
    obs_weight,
    obs_value,
    obs_error,
    loc_ids,
    loc_len,
    loc_weight,
):
    members, nodes = state.shape[1:]
    width = send_list.shape[1]
    entries = loc_ids.shape[1]
    ghosts = 2 * width
    tiles = nodes // LANES
    assert loc_ids.shape[0] == 1
    depth = depth[None]
    place = lax.axis_index("mesh").astype(jnp.int32)[None]
    work = 8 * members * nodes * nodes

    brought = [state, send_list, loc_ids, loc_weight, depth, jnp.swapaxes(coef, 0, 1), wet_faces, conn]
    brought += [obs_nodes, obs_weight, obs_value[None], obs_error[None]]
    near, far, *brought = call(
        send_flow_kernel,
        [shape(2 * members + ROWS, width)] * 2 + [shape(*a.shape, dtype=a.dtype) for a in brought],
        [place, loc_len, *brought],
        scalars=2,
        scratch=[pltpu.SemaphoreType.DMA((len(brought) + 2,))],
        raw=True,
    )
    state, send_list, loc_ids, loc_weight, depth, coef, wet_faces, conn = brought[:8]
    obs_nodes, obs_weight, obs_value, obs_error = brought[8:]
    corners = obs_nodes.shape[0]
    from_far = to_other(far)
    from_near = to_partner(near)
    big = [shape(tiles, nodes, LANES, dtype=BF16)] * 4
    small = [shape(tiles, ghosts, LANES, dtype=BF16)] * 4
    made = call(
        prepare_kernel,
        big + small + [shape(2, nodes), shape(members, nodes)],
        [place, state, coef, wet_faces, conn],
        scalars=1,
        scratch=[
            pltpu.VMEM((2, 2 * members, nodes), BF16),
            pltpu.VMEM(conn.shape, jnp.int32),
            pltpu.VMEM((2,) + conn.shape, F32),
        ],
        flops=3 * work,
    )
    operators, ghost_operators, totals, partial = made[:4], made[4:8], made[8], made[9]
    field, payload = shape(members, nodes), shape(members, width)
    early = from_near, from_far

    args = [place, state, partial, depth, from_near, from_far, *ghost_operators, send_list]
    level, far = call(level_kernel, [field, payload], args, scalars=1, flops=work)
    from_far = to_other(far)
    (near,) = call(near_picks_kernel, [payload], [place, level, send_list], scalars=1)
    from_near = to_partner(near)
    east, north = call(slope_kernel, [field] * 2, [level, *operators, totals], flops=work)
    entry_tiles = entries // LANES
    own_high, own_low, tables, found = call(
        sampling_kernel,
        [shape(entry_tiles, nodes, LANES, dtype=BF16)] * 2 + [shape(ROWS, entries), shape(ROWS, 3 * entries)],
        [place, loc_len, *early, loc_ids, loc_weight, obs_nodes, obs_weight, obs_value, obs_error],
        scalars=2,
        scratch=[
            pltpu.VMEM((ROWS, entries), jnp.int32),
            pltpu.VMEM((ROWS, entries), F32),
            pltpu.VMEM((ROWS, obs_nodes.shape[1]), F32),
        ],
        flops=work,
    )

    flow, far = call(
        flow_kernel,
        [shape(2, members, nodes), shape(2 * members, width)],
        [place, state, east, north, from_near, from_far, *ghost_operators, send_list],
        scalars=1,
        flops=work,
    )
    from_far = to_other(far)
    (near,) = call(near_picks_kernel, [shape(2 * members, width)], [place, flow, send_list], scalars=1)
    from_near = to_partner(near)
    high, low = call(
        functools.partial(others_kernel, corners),
        [shape(2 * entry_tiles, nodes, LANES, dtype=BF16)] * 2,
        [found],
        flops=work,
    )
    (partial,) = call(divergence_kernel, [field], [flow, *operators, totals], flops=work)

    payload = shape(members + ROWS, width + LANES)
    args = [place, level, partial, depth, from_near, from_far, *ghost_operators, send_list, high, low, tables]
    level, far = call(last_level_kernel, [field, payload], args, scalars=1, flops=work)
    from_far = to_other(far)
    (near,) = call(near_sums_kernel, [payload], [place, level, send_list, high, low, tables], scalars=1, flops=work)
    from_near = to_partner(near)
    east, north = call(slope_kernel, [field] * 2, [level, *operators, totals], flops=work)
    (sums,) = call(own_sums_kernel, [shape(members + ROWS, members)], [level, own_high, own_low, tables], flops=work)
    (out,) = call(
        analysis_kernel,
        [shape(3, members, nodes)],
        [flow, level, east, north, sums, from_near, from_far, *ghost_operators],
        scratch=[
            pltpu.VMEM((3, members, nodes), F32),
            pltpu.VMEM((3, 2 * members, nodes), BF16),
            pltpu.VMEM((ROWS, nodes), F32),
            pltpu.SemaphoreType.DMA((3,)),
        ],
        flops=work,
        final=True,
    )
    return out


def solution(mesh):
    spread = ("groups", "mesh")
    in_specs = (
        P(None, None, spread),
        P(spread),
        P(None, None, spread),
        P(None, spread),
        P(None, spread),
        P(None, spread),
        P(None, spread),
        P(None, spread),
        P(spread),
        P(spread),
        P(spread, None),
        P(spread),
        P(spread, None),
    )
    out_specs = P(None, None, spread)
    return jax.shard_map(local, mesh=mesh, in_specs=in_specs, out_specs=out_specs, check_vma=False)
```

```python
import functools
import math

import jax
import jax.numpy as jnp
from jax import lax
from jax.experimental import pallas as pl
from jax.experimental.pallas import tpu as pltpu
from jax.sharding import PartitionSpec as P

DT = 0.1
LANES = 128
ROWS = 8
F32 = jnp.float32
BF16 = jnp.bfloat16


def halves(value):
    high = value.astype(BF16)
    return high, (value - high.astype(F32)).astype(BF16)


def stacked(value):
    high, low = halves(value)
    return jnp.concatenate([high, low], axis=0)


def product(stack, high, low, first=0, count=None):
    rows = stack.shape[0] // 2
    count = high.shape[0] if count is None else count
    pieces = []
    for tile in range(first, first + count, 2):
        total = 0.0
        for part in (high, low):
            block = jnp.concatenate([part[tile], part[tile + 1]], axis=1)
            total = total + jnp.dot(stack, block, preferred_element_type=F32)
        pieces.append(total[:rows] + total[rows:])
    return jnp.concatenate(pieces, axis=1)


def pick_lanes(sources, indices, targets):
    rows, extent = sources.shape
    plans = []
    for index, target in zip(indices, targets):
        for start in range(0, index.shape[1], LANES):
            wide = jnp.broadcast_to(index[:, start : start + LANES], (ROWS, LANES))
            plans.append((wide & (LANES - 1), wide >> 7, target, start))

    def group(step, carry):
        first = pl.multiple_of(step * ROWS, ROWS)
        for lane, tile, (ref, row0, col0), start in plans:
            total = jnp.zeros((ROWS, LANES), F32)
            for place in range(extent // LANES):
                block = sources[pl.ds(first, ROWS), place * LANES : (place + 1) * LANES]
                found = jnp.take_along_axis(block, lane, axis=1, mode="promise_in_bounds")
                total = jnp.where(tile == place, found, total)
            ref[pl.ds(row0 + first, ROWS), col0 + start : col0 + start + LANES] = total
        return carry

    lax.fori_loop(0, rows // ROWS, group, 0, unroll=True)


def merged(targets, weights):
    targets = list(targets)
    weights = [list(group) for group in weights]
    count = len(targets)
    for first in range(count):
        for second in range(first + 1, count):
            same = targets[first] == targets[second]
            for group in weights:
                group[first] = group[first] + jnp.where(same, group[second], 0.0)
                group[second] = jnp.where(same, 0.0, group[second])
    return weights


def build_operator(targets, weights, outputs, begin, extent, tile, unroll):
    count = len(targets)
    tall = 2 * ROWS
    wanted = [jnp.broadcast_to(t - begin, (tall, LANES)).astype(jnp.int16) for t in targets]
    parts = []
    for group in weights:
        for w in group:
            high = w.astype(BF16).astype(F32)
            parts.append(
                (
                    jnp.broadcast_to(high, (tall, LANES)).astype(BF16),
                    jnp.broadcast_to(w - high, (tall, LANES)).astype(BF16),
                )
            )

    def block(step, rows):
        first = pl.multiple_of(step * tall, tall)
        values = [jnp.zeros((tall, LANES), BF16) for _ in range(2 * len(weights))]
        for slot in range(count - 1, -1, -1):
            hit = wanted[slot] == rows
            for g in range(len(weights)):
                high, low = parts[g * count + slot]
                values[2 * g] = jnp.where(hit, high, values[2 * g])
                values[2 * g + 1] = jnp.where(hit, low, values[2 * g + 1])
        for value, ref in zip(values, outputs):
            ref[tile, pl.ds(first, tall), :] = value
        return rows + jnp.int16(tall)

    start = lax.broadcasted_iota(jnp.int32, (tall, LANES), 0).astype(jnp.int16)
    lax.fori_loop(0, extent // tall, block, start, unroll=unroll)


def chosen_lists(place, lists):
    odd = place[0] & 1
    return lists[pl.ds(1 - odd, 1), :], lists[pl.ds(odd, 1), :]


def live_weight(weight, length):
    entry = lax.broadcasted_iota(jnp.int32, weight.shape, 1)
    return jnp.where(entry < length, weight, 0.0)


def send_flow_kernel(place, length, *refs):
    count = (len(refs) - 3) // 2
    held, (near, far), kept, arrived = refs[:count], refs[count : count + 2], refs[count + 2 : -1], refs[-1]
    state_at, state, lists, ids, weight = held[0], kept[0], kept[1], kept[2], kept[3]
    members, width = state.shape[1], lists.shape[1]
    pairs = [(held[1], lists), (state_at.at[1], state.at[1]), (state_at.at[2], state.at[2])]
    pairs += list(zip(held[2:], kept[2:])) + [(state_at.at[0], state.at[0])]
    copies = [pltpu.make_async_copy(a, b, arrived.at[n]) for n, (a, b) in enumerate(pairs)]
    for copy in copies:
        copy.start()
    copies[0].wait()
    chosen = chosen_lists(place, lists)
    for part in range(2):
        copies[1 + part].wait()
        pick_lanes(state.at[1 + part], chosen, [(near, part * members, 0), (far, part * members, 0)])
    for copy in copies[3:]:
        copy.wait()
    block = jnp.zeros((near.shape[0] - 2 * members, width), F32)
    row = lax.broadcasted_iota(jnp.int32, block.shape, 0)
    pieces = ids.shape[1] // width
    for at, values in enumerate((ids[...].astype(F32), live_weight(weight[...], length[0]))):
        for piece in range(pieces):
            line = values[:, piece * width : (piece + 1) * width]
            block = jnp.where(row == at * pieces + piece, jnp.broadcast_to(line, block.shape), block)
    near[2 * members :, :] = block
    far[2 * members :, :] = block


def prepare_kernel(
    place, state, coef, wet, conn, eh, el, nh, nl, geh, gel, gnh, gnl, totals, partial, stacks, targets_at, weights_at
):
    slots, nodes = conn.shape
    ghosts = geh.shape[1]
    turned = (1 - (place[0] & 1)) * (ghosts // 2)
    count = nodes // LANES
    stride = min(4 * LANES, nodes)
    for begin in range(0, nodes, stride):
        cut = slice(begin, begin + stride)
        targets = []
        for s in range(slots):
            raw = conn[s : s + 1, cut]
            ghost = raw - nodes + turned
            ghost = jnp.where(ghost >= ghosts, ghost - ghosts, ghost)
            targets.append(jnp.where(raw < nodes, raw, nodes + ghost))
        faces = [wet[s : s + 1, cut].astype(F32) for s in range(slots)]
        weights = [[faces[s] * coef[s, d : d + 1, cut] for s in range(slots)] for d in range(2)]
        for d in range(2):
            totals[d : d + 1, cut] = sum(weights[d][1:], weights[d][0])
        weights = merged(targets, weights)
        for s in range(slots):
            targets_at[s : s + 1, cut] = targets[s]
            for d in range(2):
                weights_at[d, s : s + 1, cut] = weights[d][s]

    def held(tile):
        cut = slice(tile * LANES, (tile + 1) * LANES)
        return [targets_at[s : s + 1, cut] for s in range(slots)], [
            [weights_at[d, s : s + 1, cut] for s in range(slots)] for d in range(2)
        ]

    for tile in range(count):
        build_operator(*held(tile), (eh, el, nh, nl), 0, nodes, tile, 8)
    for d in range(2):
        stacks[d] = stacked(state[1 + d])
    for tile in range(count):
        pair, d = divmod(tile, 2)
        span = slice(2 * pair * LANES, 2 * (pair + 1) * LANES)
        found = product(stacks[d], *((eh, el), (nh, nl))[d], 2 * pair, 2) - state[1 + d, :, span] * totals[d : d + 1, span]
        build_operator(*held(tile), (geh, gel, gnh, gnl), nodes, ghosts, tile, True)
        partial[:, span] = found if d == 0 else partial[:, span] + found


def ghost_flow(near, far, part, members):
    rows = slice(part * members, (part + 1) * members)
    return jnp.concatenate([near[rows, :], far[rows, :]], axis=1)


def stepped_level(held, partial, depth, near, far, geh, gel, gnh, gnl):
    level = held.at[0] if len(held.shape) == 3 else held
    members = level.shape[0]
    divergence = (
        partial[...]
        + product(stacked(ghost_flow(near, far, 0, members)), geh, gel)
        + product(stacked(ghost_flow(near, far, 1, members)), gnh, gnl)
    )
    return level[...] - DT * depth[...] * divergence


def level_kernel(place, held, partial, depth, near, far, geh, gel, gnh, gnl, lists, new_level, to_far):
    new_level[...] = stepped_level(held, partial, depth, near, far, geh, gel, gnh, gnl)
    pick_lanes(new_level, chosen_lists(place, lists)[1:], [(to_far, 0, 0)])


def near_picks_kernel(place, field, lists, to_near):
    chosen = chosen_lists(place, lists)[:1]
    if len(field.shape) == 2:
        pick_lanes(field, chosen, [(to_near, 0, 0)])
    else:
        for part in range(field.shape[0]):
            pick_lanes(field.at[part], chosen, [(to_near, part * field.shape[1], 0)])


def thirds(value):
    high, rest = halves(value)
    middle = rest
    low = (value - high.astype(F32) - middle.astype(F32)).astype(BF16)
    return high, middle, low


def row_products(left, right):
    rows = left.shape[0]
    ours, theirs = thirds(left), thirds(right)
    total = 0.0
    for skip, part in enumerate(theirs):
        block = jnp.concatenate(ours[: 3 - skip], axis=0)
        found = lax.dot_general(block, part, (((1,), (1,)), ((), ())), preferred_element_type=F32)
        sums = [found[at * rows : (at + 1) * rows] for at in range(3 - skip)]
        while len(sums) > 1:
            sums[-2:] = [sums[-2] + sums[-1]]
        total = sums[0] + total
    return total


def list_sums(seen, value, weight):
    obs_mean = jnp.mean(seen, axis=0, keepdims=True)
    anomalies = seen - obs_mean
    pull = jnp.broadcast_to(weight * (value - obs_mean), (ROWS, seen.shape[1]))
    left = jnp.concatenate([anomalies * weight, pull], axis=0)
    return row_products(left, anomalies)


def neighbour_payload(which, place, level, lists, high, low, tables, ref):
    members, width = level.shape[0], lists.shape[1]
    tiles = high.shape[0] // 2
    pick_lanes(level, [chosen_lists(place, lists)[which]], [(ref, 0, 0)])
    seen = product(stacked(level[...]), high, low, which * tiles, tiles)
    sums = list_sums(seen, tables[2 * which : 2 * which + 1, :], tables[2 * which + 1 : 2 * which + 2, :])
    ref[members:, :width] = jnp.zeros((ROWS, width), F32)
    ref[:, width:] = jnp.concatenate([sums, jnp.zeros((members + ROWS, LANES - members), F32)], axis=1)


def last_level_kernel(
    place, held, partial, depth, near, far, geh, gel, gnh, gnl, lists, high, low, tables, new_level, to_far
):
    new_level[...] = stepped_level(held, partial, depth, near, far, geh, gel, gnh, gnl)
    neighbour_payload(1, place, new_level, lists, high, low, tables, to_far)


def near_sums_kernel(place, level, lists, high, low, tables, to_near):
    neighbour_payload(0, place, level, lists, high, low, tables, to_near)


def slope_kernel(level, eh, el, nh, nl, totals, east, north):
    stack = stacked(level[...])
    east[...] = product(stack, eh, el) - level[...] * totals[0:1, :]
    north[...] = product(stack, nh, nl) - level[...] * totals[1:2, :]


def sampling_kernel(
    place, length, near, far, ids, weight, obs_nodes, obs_weight, obs_value, obs_error, high, low, tables, found,
    numbers, strengths, scratch,
):
    entries, width = ids.shape[1], near.shape[1]
    corners, obs_count = obs_nodes.shape
    base = place[0] * obs_count
    scratch[0:corners, :] = obs_nodes[...].astype(F32)
    scratch[corners : 2 * corners, :] = obs_weight[...]
    scratch[2 * corners : 2 * corners + 1, :] = obs_value[...]
    scratch[2 * corners + 1 : 2 * corners + 2, :] = 1.0 / (obs_error[...] * obs_error[...])
    first = near.shape[0] - ROWS
    pieces = entries // width
    for piece in range(pieces):
        cut = slice(piece * width, (piece + 1) * width)
        for owner, ref in enumerate((near, far)):
            at = first + piece
            numbers[owner : owner + 1, cut] = ref[at : at + 1, :].astype(jnp.int32)
            strengths[owner : owner + 1, cut] = ref[at + pieces : at + pieces + 1, :]
    numbers[2:3, :] = ids[...]
    strengths[2:3, :] = live_weight(weight[...], length[0])
    tiles = entries // LANES
    places = [(owner, tile) for owner in range(3) for tile in range(tiles)]
    kept = {}
    for owner, tile in places:
        index = numbers[owner : owner + 1, tile * LANES : (tile + 1) * LANES] - base
        own = (index >= 0) & (index < obs_count)
        kept[owner, tile] = own, jnp.where(own, index, 0)
    pick_lanes(
        scratch,
        [kept[spot][1] for spot in places],
        [(found, 0, (owner * tiles + tile) * LANES) for owner, tile in places],
    )
    for owner, tile in places:
        at = slice((owner * tiles + tile) * LANES, (owner * tiles + tile + 1) * LANES)
        own = kept[owner, tile][0]
        cut = slice(tile * LANES, (tile + 1) * LANES)
        found[corners : 2 * corners, at] = jnp.where(own, found[corners : 2 * corners, at], 0.0)
        force = found[2 * corners + 1 : 2 * corners + 2, at] * strengths[owner : owner + 1, cut]
        tables[2 * owner : 2 * owner + 1, cut] = found[2 * corners : 2 * corners + 1, at]
        tables[2 * owner + 1 : 2 * owner + 2, cut] = jnp.where(own, force, 0.0)
    corner_operator(found, 2 * tiles, corners, high, low)


def corner_operator(found, first, corners, high, low):
    for tile in range(high.shape[0]):
        here = found[:, (first + tile) * LANES : (first + tile + 1) * LANES]
        targets = [here[c : c + 1, :].astype(jnp.int32) for c in range(corners)]
        shares = [here[corners + c : corners + c + 1, :] for c in range(corners)]
        build_operator(targets, merged(targets, [shares]), (high, low), 0, high.shape[1], tile, 32)


def others_kernel(corners, found, high, low):
    corner_operator(found, 0, corners, high, low)


def flow_kernel(place, flow, east, north, near, far, geh, gel, gnh, gnl, lists, new_flow, to_far):
    members = east.shape[0]
    stack = stacked(jnp.concatenate([near[...], far[...]], axis=1))
    chosen = chosen_lists(place, lists)[1:]
    first = flow.shape[0] - 2
    new_flow[0] = flow[first] - DT * (east[...] + product(stack, geh, gel))
    new_flow[1] = flow[first + 1] - DT * (north[...] + product(stack, gnh, gnl))
    for part in range(2):
        pick_lanes(new_flow.at[part], chosen, [(to_far, part * members, 0)])


def divergence_kernel(flow, eh, el, nh, nl, totals, partial):
    first = flow.shape[0] - 2
    east, north = flow[first], flow[first + 1]
    partial[...] = (
        product(stacked(east), eh, el)
        + product(stacked(north), nh, nl)
        - east * totals[0:1, :]
        - north * totals[1:2, :]
    )


def last_slope_kernel(level, eh, el, nh, nl, totals, high, low, tables, east, north, sums):
    slope_kernel(level, eh, el, nh, nl, totals, east, north)
    sums[...] = list_sums(product(stacked(level[...]), high, low), tables[4:5, :], tables[5:6, :])


def pair_inverse(a, b, c):
    r = 1.0 / (a * c - b * b)
    return c * r, -(b * r), a * r


def pair_rows(a, b, c, first, second):
    m = b / a
    return first * lax.rsqrt(a), (second - m * first) * lax.rsqrt(c - m * b)


def inverse_factor(gram, beside):
    size = gram.shape[0]
    wide = (ROWS, 2 * size)
    row = lax.broadcasted_iota(jnp.int32, (size, size), 0)
    col = lax.broadcasted_iota(jnp.int32, (size, size), 1)
    table = jnp.concatenate([gram, (row == col).astype(F32)], axis=1)
    blocks = [table[b : b + ROWS, :] for b in range(0, size, ROWS)]
    inner = lax.broadcasted_iota(jnp.int32, wide, 0)

    def spread(value):
        return jnp.broadcast_to(value, wide)

    def columns_of(block, pivot):
        return [spread(block[:, pivot + i : pivot + i + 1]) for i in range(ROWS)]

    done = []
    for home in range(len(blocks)):
        pivot = home * ROWS
        lines = [spread(blocks[home][i : i + 1, :]) for i in range(ROWS)]
        columns = columns_of(blocks[home], pivot)
        entry = {(i, j): spread(columns[j][i : i + 1, :]) for i in range(ROWS) for j in range(i + 1)}
        inverses, factors = {}, {}
        result = jnp.zeros(wide, F32)
        for k in range(0, ROWS, 2):
            head = entry[k, k], entry[k + 1, k], entry[k + 1, k + 1]
            p = inverses[k] = pair_inverse(*head)
            for i, value in enumerate(pair_rows(*head, lines[k], lines[k + 1])):
                result = jnp.where(inner == k + i, value, result)
            for r in range(k + 2, ROWS):
                u, v = entry[r, k], entry[r, k + 1]
                t = factors[r, k] = u * p[0] + v * p[1], u * p[1] + v * p[2]
                for c in range(k + 2, r + 1):
                    entry[r, c] = entry[r, c] - (t[0] * entry[c, k] + t[1] * entry[c, k + 1])
                lines[r] = lines[r] - (t[0] * lines[k] + t[1] * lines[k + 1])
        done.append(result)
        z = [None] * ROWS
        for k in range(ROWS - 2, -1, -2):
            p = inverses[k]
            z[k] = p[0] * lines[k] + p[1] * lines[k + 1]
            z[k + 1] = p[1] * lines[k] + p[2] * lines[k + 1]
            for r in range(k + 2, ROWS):
                z[k] = z[k] - factors[r, k][0] * z[r]
                z[k + 1] = z[k + 1] - factors[r, k][1] * z[r]
        for place in range(home + 1, len(blocks)):
            terms = [f * z[i] for i, f in enumerate(columns_of(blocks[place], pivot))]
            while len(terms) > 1:
                terms = [terms[i] + terms[i + 1] for i in range(0, len(terms), 2)]
            blocks[place] = blocks[place] - terms[0]
        beside()
    return jnp.concatenate(done, axis=0)[:, size:]


def analysis_kernel(
    flow, level, east, north, sums, near, far, geh, gel, gnh, gnl, out, result, moved, averages, sent
):
    members, nodes = level.shape
    width = near.shape[1] - LANES
    total = sums[...] + near[:, width : width + members] + far[:, width : width + members]
    row = lax.broadcasted_iota(jnp.int32, (members, members), 0)
    col = lax.broadcasted_iota(jnp.int32, (members, members), 1)
    gram = total[:members] + jnp.where(row == col, members - 1.0, 0.0)
    rhs = total[members : members + 1]
    stack = stacked(jnp.concatenate([near[:members, :width], far[:members, :width]], axis=1))
    operators = ((geh, gel), (gnh, gnl))

    def piece(part, tile):
        cut = slice(tile * LANES, (tile + 2) * LANES)
        if part == 0:
            field = level[:, cut]
        else:
            slope = (east, north)[part - 1][:, cut] + product(stack, *operators[part - 1], tile, 2)
            field = flow[part - 1, :, cut] - DT * slope
        average = jnp.mean(field, axis=0, keepdims=True)
        moved[part, :, cut] = stacked(field - average)
        averages[part : part + 1, cut] = average

    pieces = [(part, tile) for part in (1, 2, 0) for tile in range(0, nodes // LANES, 2)]

    def beside():
        for _ in range(2):
            if pieces:
                piece(*pieces.pop(0))

    inverse = inverse_factor(gram, beside)
    while pieces:
        beside()
    halfway = jnp.sum(inverse * rhs, axis=1, keepdims=True)
    mean_w = jnp.sum(inverse * halfway, axis=0, keepdims=True)
    blend = math.sqrt(members - 1.0) * inverse + mean_w
    blend = stacked(jnp.concatenate([blend, blend], axis=1))
    copies = []
    for part in range(3):
        change = jnp.dot(blend, moved[part], preferred_element_type=F32)
        result[part] = averages[part : part + 1, :] + (change[:members] + change[members:])
        copies.append(pltpu.make_async_copy(result.at[part], out.at[part], sent.at[part]))
        copies[-1].start()
    for copy in copies:
        copy.wait()


def call(kernel, outs, args, scalars=0, scratch=(), flops=0, final=False, limit=16, raw=False):
    vmem = pl.BlockSpec(memory_space=pltpu.VMEM)
    in_specs = [pl.BlockSpec(memory_space=pltpu.SMEM)] * scalars + [pl.BlockSpec(memory_space=pltpu.HBM) if raw else vmem] * (len(args) - scalars)
    held = sum(math.prod(a.shape) * a.dtype.itemsize for a in list(args) + list(outs))
    if not final:
        outs = [pltpu.VMEM(o.shape, o.dtype) for o in outs]
    space = pltpu.HBM if raw else pltpu.VMEM
    args = list(args[:scalars]) + [pltpu.with_memory_space_constraint(a, space) for a in args[scalars:]]
    return pl.pallas_call(
        kernel,
        out_shape=outs,
        in_specs=in_specs,
        out_specs=[pl.BlockSpec(memory_space=pltpu.HBM) if final else vmem] * len(outs),
        scratch_shapes=scratch,
        compiler_params=pltpu.CompilerParams(vmem_limit_bytes=limit << 20),
        cost_estimate=pl.CostEstimate(flops=flops, bytes_accessed=held, transcendentals=0),
    )(*args)


def shape(*dims, dtype=F32):
    return jax.ShapeDtypeStruct(dims, dtype)


def to_partner(value):
    pairs = [(i, i ^ 1) for i in range(lax.axis_size("mesh"))]
    return lax.ppermute(value, "mesh", pairs)


def to_other(value):
    count = lax.axis_size("mesh")
    others = [(i, ((i + 1) ^ 1) - 1) for i in range(1, count - 1)]
    return lax.ppermute(value, "mesh", others)


def local(
    state,
    depth,
    coef,
    wet_faces,
    conn,
    send_list,
    obs_nodes,
    obs_weight,
    obs_value,
    obs_error,
    loc_ids,
    loc_len,
    loc_weight,
):
    members, nodes = state.shape[1:]
    width = send_list.shape[1]
    entries = loc_ids.shape[1]
    ghosts = 2 * width
    tiles = nodes // LANES
    assert loc_ids.shape[0] == 1
    depth = depth[None]
    place = lax.axis_index("mesh").astype(jnp.int32)[None]
    work = 8 * members * nodes * nodes

    brought = [state, send_list, loc_ids, loc_weight, depth, jnp.swapaxes(coef, 0, 1), wet_faces, conn]
    brought += [obs_nodes, obs_weight, obs_value[None], obs_error[None]]
    near, far, *brought = call(
        send_flow_kernel,
        [shape(2 * members + ROWS, width)] * 2 + [shape(*a.shape, dtype=a.dtype) for a in brought],
        [place, loc_len, *brought],
        scalars=2,
        scratch=[pltpu.SemaphoreType.DMA((len(brought) + 2,))],
        raw=True,
    )
    state, send_list, loc_ids, loc_weight, depth, coef, wet_faces, conn = brought[:8]
    obs_nodes, obs_weight, obs_value, obs_error = brought[8:]
    corners = obs_nodes.shape[0]
    from_far = to_other(far)
    from_near = to_partner(near)
    big = [shape(tiles, nodes, LANES, dtype=BF16)] * 4
    small = [shape(tiles, ghosts, LANES, dtype=BF16)] * 4
    made = call(
        prepare_kernel,
        big + small + [shape(2, nodes), shape(members, nodes)],
        [place, state, coef, wet_faces, conn],
        scalars=1,
        scratch=[
            pltpu.VMEM((2, 2 * members, nodes), BF16),
            pltpu.VMEM(conn.shape, jnp.int32),
            pltpu.VMEM((2,) + conn.shape, F32),
        ],
        flops=3 * work,
    )
    operators, ghost_operators, totals, partial = made[:4], made[4:8], made[8], made[9]
    field, payload = shape(members, nodes), shape(members, width)
    early = from_near, from_far

    args = [place, state, partial, depth, from_near, from_far, *ghost_operators, send_list]
    level, far = call(level_kernel, [field, payload], args, scalars=1, flops=work)
    from_far = to_other(far)
    (near,) = call(near_picks_kernel, [payload], [place, level, send_list], scalars=1)
    from_near = to_partner(near)
    east, north = call(slope_kernel, [field] * 2, [level, *operators, totals], flops=work)
    entry_tiles = entries // LANES
    own_high, own_low, tables, found = call(
        sampling_kernel,
        [shape(entry_tiles, nodes, LANES, dtype=BF16)] * 2 + [shape(ROWS, entries), shape(ROWS, 3 * entries)],
        [place, loc_len, *early, loc_ids, loc_weight, obs_nodes, obs_weight, obs_value, obs_error],
        scalars=2,
        scratch=[
            pltpu.VMEM((ROWS, entries), jnp.int32),
            pltpu.VMEM((ROWS, entries), F32),
            pltpu.VMEM((ROWS, obs_nodes.shape[1]), F32),
        ],
        flops=work,
    )

    flow, far = call(
        flow_kernel,
        [shape(2, members, nodes), shape(2 * members, width)],
        [place, state, east, north, from_near, from_far, *ghost_operators, send_list],
        scalars=1,
        flops=work,
    )
    from_far = to_other(far)
    (near,) = call(near_picks_kernel, [shape(2 * members, width)], [place, flow, send_list], scalars=1)
    from_near = to_partner(near)
    high, low = call(
        functools.partial(others_kernel, corners),
        [shape(2 * entry_tiles, nodes, LANES, dtype=BF16)] * 2,
        [found],
        flops=work,
    )
    (partial,) = call(divergence_kernel, [field], [flow, *operators, totals], flops=work)

    payload = shape(members + ROWS, width + LANES)
    args = [place, level, partial, depth, from_near, from_far, *ghost_operators, send_list, high, low, tables]
    level, far = call(last_level_kernel, [field, payload], args, scalars=1, flops=work)
    from_far = to_other(far)
    (near,) = call(near_sums_kernel, [payload], [place, level, send_list, high, low, tables], scalars=1, flops=work)
    from_near = to_partner(near)
    east, north, sums = call(
        last_slope_kernel,
        [field] * 2 + [shape(members + ROWS, members)],
        [level, *operators, totals, own_high, own_low, tables],
        flops=work,
    )
    (out,) = call(
        analysis_kernel,
        [shape(3, members, nodes)],
        [flow, level, east, north, sums, from_near, from_far, *ghost_operators],
        scratch=[
            pltpu.VMEM((3, members, nodes), F32),
            pltpu.VMEM((3, 2 * members, nodes), BF16),
            pltpu.VMEM((ROWS, nodes), F32),
            pltpu.SemaphoreType.DMA((3,)),
        ],
        flops=work,
        final=True,
    )
    return out


def solution(mesh):
    spread = ("groups", "mesh")
    in_specs = (
        P(None, None, spread),
        P(spread),
        P(None, None, spread),
        P(None, spread),
        P(None, spread),
        P(None, spread),
        P(None, spread),
        P(None, spread),
        P(spread),
        P(spread),
        P(spread, None),
        P(spread),
        P(spread, None),
    )
    out_specs = P(None, None, spread)
    return jax.shard_map(local, mesh=mesh, in_specs=in_specs, out_specs=out_specs, check_vma=False)
```
